32 devices in a mesh: lat: 8 (over y, x, core), chan: 4 (over z).
Axes of the slice: x: 2, y: 2, z: 4, core: 2. Of those that a mesh axis runs over, the one named last changes fastest.
Arguments:
- atmosphere: bfloat16 [256, 64, 1536], P('chan', 'lat'), may hold values from -6 to 6
- first_weight: bfloat16 [256, 16, 5, 5], P('chan'), may hold values from -0.3125 to 0.3125
- first_bias: float32 [256], P('chan'), may hold values from -3 to 3
- second_weight: bfloat16 [256, 16, 5, 5], P('chan'), may hold values from -0.3125 to 0.3125
Outputs:
- spectrum: float32 [128, 2, 256, 2, 128], P('lat', None, 'chan')
The draws below stay inside these ranges and needn't reach their ends.
All inputs are finite; a program needn't handle non-finite values.
Results may differ from the reference program's by a relative error of at most 0.007.
Values may be sent and summed in bfloat16 or wider, within the bound.
No kernel may reach another device: no remote copies, remote signals or barrier semaphores. Data moves between devices by JAX's collectives and lax.ppermute only.
A program may use at most 128 MiB of HBM per device.

```python
import math
import jax
import jax.numpy as jnp
from jax import lax

CHANNELS = 256
GROUP = 16
KERNEL = 5
LON = 1536
ORDERS = 128
DEGREES = 256
LAT = 64


def block_scale(rng, extent, split, least, high):
    gain = 1.0
    for axis_at, blocks in split:
        steps = jax.random.uniform(jax.random.fold_in(jax.random.fold_in(rng, 6), axis_at), (blocks,), jnp.float32, least / len(split), high / len(split))
        gain = gain * jnp.repeat(jnp.exp(steps), extent[axis_at] // blocks).reshape((-1,) + (1,) * (len(extent) - 1 - axis_at))
    return gain


def centred(key, extent, scale, most, split=(), held_as=jnp.bfloat16):
    drawn = scale * jax.random.normal(key, extent, jnp.float32)
    if split:
        drawn = drawn * block_scale(key, extent, split, -0.22, 0.18)
    return jnp.clip(drawn, -most, most).astype(held_as)


def setup_inputs(seed: int = 0) -> dict:
    seeds = jax.random.split(jax.random.key(seed), 5)
    atmosphere = centred(seeds[0], (CHANNELS, LAT, LON), 1.0, 6.0, ((0, 4), (1, 8)))
    first_weight = centred(seeds[1], (CHANNELS, GROUP, KERNEL, KERNEL), (GROUP * KERNEL * KERNEL) ** -0.5, 0.3125, ((0, 4),))
    first_bias = centred(seeds[2], (CHANNELS,), 0.5, 3.0, ((0, 4),), jnp.float32)
    second_weight = centred(seeds[3], (CHANNELS, GROUP, KERNEL, KERNEL), (GROUP * KERNEL * KERNEL) ** -0.5, 0.3125, ((0, 4),))
    return {"atmosphere": atmosphere, "first_weight": first_weight, "first_bias": first_bias, "second_weight": second_weight}


def fourier_table(length, orders):
    places = lax.broadcasted_iota(jnp.int32, (length, orders), 0)
    numbers = lax.broadcasted_iota(jnp.int32, (length, orders), 1) + 1
    phases = (places * numbers % length).astype(jnp.float32) * (2.0 * math.pi / length)
    factor = 1.0 / math.sqrt(length)
    return (jnp.concatenate([jnp.cos(phases), -jnp.sin(phases)], axis=1) * factor).astype(jnp.bfloat16)

def legendre(colatitude, orders, degrees):
    cosine = jnp.cos(colatitude)[None, :]
    sines = jnp.sin(colatitude)[None, :]
    order_real = orders.astype(jnp.float32)[:, None]
    log_diag = 0.5 * (jnp.log((2.0 * order_real + 1.0) / 2.0) + lax.lgamma(2.0 * order_real + 1.0) - order_real * math.log(4.0) - 2.0 * lax.lgamma(order_real + 1.0)) + order_real * jnp.log(sines)
    diagonal = jnp.exp(log_diag)
    empty_rows = jnp.zeros_like(diagonal)

    def advance(carried, degree):
        latest, before = carried
        degree_real = degree.astype(jnp.float32)
        spread = jnp.maximum(degree_real * degree_real - order_real * order_real, 1.0)
        raising = jnp.sqrt(jnp.maximum(4.0 * degree_real * degree_real - 1.0, 1.0) / spread)
        previous = degree_real - 1.0
        lowering = jnp.sqrt(jnp.maximum(previous * previous - order_real * order_real, 0.0) / jnp.maximum(4.0 * previous * previous - 1.0, 1.0))
        raised = raising * (cosine * latest - lowering * before)
        result = jnp.where(degree_real == order_real, diagonal, jnp.where(degree_real > order_real, raised, 0.0))
        return ((result, latest), result)
    _, stacked = lax.scan(advance, (empty_rows, empty_rows), jnp.arange(degrees, dtype=jnp.int32), unroll=16)
    return stacked

def weighted_table(north_rows, orders, total_rows, degrees):
    colatitude = math.pi * (north_rows.astype(jnp.float32) + 0.5) / total_rows
    quadrature = math.pi * jnp.sin(colatitude) / math.sqrt(total_rows)
    return legendre(colatitude, orders, degrees) * quadrature[None, None, :]

def project_exact(even_sum, odd_sum, stacked, orders):
    degrees, number, height = stacked.shape
    paired = stacked.reshape(degrees // 2, 2, number, height).transpose(2, 1, 3, 0).astype(jnp.bfloat16)
    parity = (orders[:, None] + jnp.arange(2, dtype=jnp.int32)[None, :]) % 2 == 0
    selected = jnp.where(parity, even_sum[..., None], odd_sum[..., None])
    return jnp.einsum('crakq,kqrj->kqcaj', selected.astype(jnp.float32), paired.astype(jnp.float32), precision=lax.Precision.HIGHEST)

def convolve(padded, kernel):
    radius = kernel.shape[3] // 2
    widened = jnp.concatenate([padded[..., -radius:], padded, padded[..., :radius]], axis=2)
    result = lax.conv_general_dilated(widened[None], kernel, (1, 1), 'VALID', feature_group_count=padded.shape[0] // kernel.shape[1], precision=lax.Precision.HIGHEST)
    return result[0]

def reference(atmosphere, first_weight, first_bias, second_weight):
    halfway = LAT // 2
    radius = KERNEL // 2
    groups = CHANNELS // GROUP
    fourier = fourier_table(LON, ORDERS)
    orders = jnp.arange(1, ORDERS + 1, dtype=jnp.int32)
    spherical = weighted_table(jnp.arange(halfway, dtype=jnp.int32), orders, LAT, DEGREES)

    def per_group(pieces):
        group_block, kernel_one, offsets, kernel_two = pieces
        inputs = group_block.astype(jnp.float32)
        padded = jnp.pad(inputs, ((0, 0), (radius, radius), (0, 0)))
        hidden = jax.nn.gelu(convolve(padded, kernel_one.astype(jnp.float32)) + offsets[:, None, None], approximate=False).astype(jnp.bfloat16)
        padded = jnp.pad(hidden.astype(jnp.float32), ((0, 0), (radius, radius), (0, 0)))
        updated = (inputs + convolve(padded, kernel_two.astype(jnp.float32))).astype(jnp.bfloat16)
        spectra = jnp.dot(updated.reshape(GROUP * LAT, LON), fourier, preferred_element_type=jnp.float32)
        spectra = spectra.astype(jnp.bfloat16).reshape(GROUP, LAT, 2, ORDERS)
        northern = spectra[:, :halfway].astype(jnp.float32)
        southern = spectra[:, halfway:][:, ::-1].astype(jnp.float32)
        even_sum = (northern + southern).astype(jnp.bfloat16)
        odd_sum = (northern - southern).astype(jnp.bfloat16)
        return project_exact(even_sum, odd_sum, spherical, orders)
    stacked = lax.map(per_group, (atmosphere.reshape(groups, GROUP, LAT, LON), first_weight.reshape(groups, GROUP, GROUP, KERNEL, KERNEL), first_bias.reshape(groups, GROUP), second_weight.reshape(groups, GROUP, GROUP, KERNEL, KERNEL)))
    return stacked.transpose(1, 2, 0, 3, 4, 5).reshape(ORDERS, 2, CHANNELS, 2, DEGREES // 2)
```

```python
import math

import jax
import jax.numpy as jnp
import numpy as np
from jax import lax
from jax.experimental import pallas as pl
from jax.experimental.pallas import tpu as pltpu
from jax.sharding import PartitionSpec as P

ORDERS = 128
DEGREES = 256
VMEM_BYTES = 40 * 2**20
LANES = 128
F32 = jnp.float32
BF16 = jnp.bfloat16


def dot_tn(left, right):
    return lax.dot_general(left, right, (((0,), (0,)), ((), ())), preferred_element_type=F32)


def dot_nt(left, right):
    return lax.dot_general(left, right, (((1,), (1,)), ((), ())), preferred_element_type=F32)


def dot_nn(left, right):
    return jnp.dot(left, right, preferred_element_type=F32)


def iota(shape, dim):
    return lax.broadcasted_iota(jnp.int32, shape, dim)


def gelu(value):
    return 0.5 * value * (1.0 + lax.erf(value * math.sqrt(0.5)))


def call(kernel, name, out_shape, scratch, flops, args, grid=None, in_specs=None, out_specs=None):
    whole = pl.BlockSpec(memory_space=pltpu.VMEM)
    extra = {} if grid is None else {"grid": grid}
    size = sum(math.prod(a.shape) * a.dtype.itemsize for a in (*args, *jax.tree.leaves(out_shape)))
    return pl.pallas_call(
        kernel,
        out_shape=out_shape,
        in_specs=in_specs or [whole] * len(args),
        out_specs=out_specs or jax.tree.map(lambda _: whole, out_shape),
        scratch_shapes=scratch,
        compiler_params=pltpu.CompilerParams(vmem_limit_bytes=VMEM_BYTES),
        cost_estimate=pl.CostEstimate(flops=flops, transcendentals=0, bytes_accessed=size),
        name=name,
        **extra,
    )(*args)


def turned(number, length):
    number = number.astype(F32)
    number = number - length * jnp.floor(number / length)
    return number * (2.0 * math.pi / length)


def write_fourier(fourier_ref, length, orders):
    tile = 128
    factor = 1.0 / math.sqrt(length)
    shape = (tile, orders)
    fine = turned(iota(shape, 0) * (iota(shape, 1) + 1), length)
    fine_cos, fine_sin = jnp.cos(fine), jnp.sin(fine)
    blocks = length // tile
    padded = -(-blocks // 8) * 8
    shape = (padded, orders)
    coarse = turned(iota(shape, 0) * tile * (iota(shape, 1) + 1), length)
    coarse_cos, coarse_sin = jnp.cos(coarse) * factor, jnp.sin(coarse) * factor
    for block in range(blocks):
        cosine = coarse_cos[block : block + 1, :]
        sine = coarse_sin[block : block + 1, :]
        rows = slice(block * tile, (block + 1) * tile)
        fourier_ref[rows, :orders] = (cosine * fine_cos - sine * fine_sin).astype(BF16)
        fourier_ref[rows, orders:] = (-(sine * fine_cos + cosine * fine_sin)).astype(BF16)


def write_spectra(send_ref, slot, real, imaginary):
    members, _, owned, _ = send_ref.shape
    flipped = jnp.concatenate([real, imaginary], axis=0).T
    for device in range(members):
        send_ref[device, slot] = flipped[device * owned : (device + 1) * owned, :].astype(BF16)


def taps_of(weight_ref, dx):
    return jnp.concatenate([weight_ref[dy, dx] for dy in range(weight_ref.shape[0])], axis=0)


def shifted_sum(partial_ref, rows, height, first, count):
    taps = rows // height
    radius = taps // 2
    total = None
    for dx in range(taps):
        start = dx * height + first
        piece = partial_ref[start : start + count, :]
        if dx != radius:
            piece = pltpu.roll(piece, (radius - dx) % piece.shape[1], 1)
        total = piece if total is None else total + piece
    return total


def interior_kernel(
    group, weight_ref, bias_ref, field_ref,
    edge_ref, rim_ref, fourier_ref, send_field_ref, send_hidden_ref,
    band_ref, partial_ref, hidden_ref, spectra_ref,
):
    taps = weight_ref.shape[0]
    radius = taps // 2
    channels = weight_ref.shape[3]
    groups = channels // group
    length = field_ref.shape[1]
    height = field_ref.shape[0] // channels
    orders = fourier_ref.shape[1] // 2
    inner = height - 2 * radius
    block = height * group
    rows = taps * block

    write_fourier(fourier_ref, length, orders)
    shape = (taps * group, height * block)
    place = iota(shape, 0)
    column = iota(shape, 1)
    out_row, column = column // block, column % block
    chosen = (place % group == column // height) & (place // group == column % height - out_row + radius)
    selector = chosen.astype(F32).astype(BF16)
    rim_shape = (taps * group, radius * group)
    rim_place = iota(rim_shape, 0)
    rim_column = iota(rim_shape, 1)
    same = rim_place % group == rim_column // radius
    rim_row = rim_column % radius
    rim_rows = taps * radius * group
    for dx in range(taps):
        mine = taps_of(weight_ref, dx)
        spread = dot_tn(mine, selector).astype(BF16)
        for g in range(groups):
            for row in range(height):
                start = g * rows + dx * block + row * group
                band_ref[start : start + group, :] = spread[
                    g * group : (g + 1) * group, row * block : (row + 1) * block
                ]
        for side in range(2):
            for row in range(radius):
                tap = rim_row - row + (0 if side == 0 else taps - 1)
                pick = (same & (rim_place // group == tap)).astype(F32).astype(BF16)
                spread = dot_tn(mine, pick).astype(BF16)
                for g in range(groups):
                    start = (g * 2 + side) * rim_rows + (dx * radius + row) * group
                    rim_ref[start : start + group, :] = spread[g * group : (g + 1) * group, :]

    def per_group(g, carry):
        band = band_ref[pl.ds(pl.multiple_of(g * rows, 16), rows), :]
        field = field_ref[pl.ds(pl.multiple_of(g * block, 16), block), :]
        partial_ref[...] = dot_nn(band, field)
        mine = pl.ds(pl.multiple_of(g * group, 16), group)
        bias = bias_ref[mine, :][:, :1]
        for row in range(height):
            total = shifted_sum(partial_ref, rows, block, row * group, group) + bias
            if radius <= row < height - radius:
                start = pl.multiple_of((row - radius) * channels + g * group, 16)
                hidden_ref[pl.ds(start, group), :] = gelu(total).astype(BF16)
            else:
                edge_ref[row if row < radius else row - inner, mine, :] = total
        return carry

    lax.fori_loop(0, groups, per_group, 0)

    found = dot_nn(field_ref[...], fourier_ref[...])
    total = height * channels
    for part in range(2):
        spectra_ref[part * total : (part + 1) * total, :] = found[:, part * orders : (part + 1) * orders]
    for row in range(height):
        real, imaginary = (
            spectra_ref[pl.ds(part * total + row, channels, stride=height), :] for part in range(2)
        )
        write_spectra(send_field_ref, row, real, imaginary)
    found = dot_nn(hidden_ref[...], fourier_ref[...])
    for row in range(inner):
        mine = found[row * channels : (row + 1) * channels, :]
        write_spectra(send_hidden_ref, row, mine[:, :orders], mine[:, orders:])


def rim_kernel(
    group, radius, rim_ref, edge_ref, before_ref, after_ref, fourier_ref,
    send_ref, partial_ref, hidden_ref,
):
    channels = edge_ref.shape[1]
    groups = channels // group
    orders = fourier_ref.shape[1] // 2
    rows = partial_ref.shape[0]
    depth = radius * group

    def per_group(g, carry):
        for side, halo_ref in enumerate((before_ref, after_ref)):
            rim = rim_ref[pl.ds(pl.multiple_of((g * 2 + side) * rows, 16), rows), :]
            halo = halo_ref[pl.ds(pl.multiple_of(g * depth, 16), depth), :]
            partial_ref[...] = dot_nn(rim, halo)
            for row in range(radius):
                total = shifted_sum(partial_ref, rows, depth, row * group, group)
                place = side * radius + row
                total = total + edge_ref[place, pl.ds(pl.multiple_of(g * group, 16), group), :]
                start = pl.multiple_of(place * channels + g * group, 16)
                hidden_ref[pl.ds(start, group), :] = gelu(total).astype(BF16)
        return carry

    lax.fori_loop(0, groups, per_group, 0)
    found = dot_nn(hidden_ref[...], fourier_ref[...])
    for row in range(2 * radius):
        mine = found[row * channels : (row + 1) * channels, :]
        write_spectra(send_ref, row, mine[:, :orders], mine[:, orders:])


def tables_kernel(group, turn_ref, sphere_ref, weight_ref, legendre_ref, mixing_ref, steps_ref, base_ref):
    taps = weight_ref.shape[0]
    radius = taps // 2
    channels = weight_ref.shape[3]
    owned, degrees, places = legendre_ref.shape
    wide = 2 * channels
    tiles = places // LANES
    first_order = lax.axis_index("lat") * owned + 1

    shape = (owned, places)
    order = (iota(shape, 0) + first_order).astype(F32)
    square = order * order
    cosine = jnp.broadcast_to(sphere_ref[0:1, :], shape)
    log_sine = jnp.broadcast_to(sphere_ref[1:2, :], shape)
    quadrature = jnp.broadcast_to(sphere_ref[2:3, :], shape)
    counts = (owned, ORDERS)
    number = (iota(counts, 1) + 1).astype(F32)
    ratio = jnp.where(
        iota(counts, 1) < iota(counts, 0) + first_order, jnp.log((2.0 * number - 1.0) / (2.0 * number)), 0.0
    )
    log_ratio = jnp.sum(ratio, axis=1, keepdims=True)
    diagonal = jnp.exp(0.5 * (jnp.log((2.0 * order + 1.0) / 2.0) + log_ratio) + order * log_sine)

    def advance(degree, carried):
        latest, before = carried
        real = jnp.full(shape, degree, jnp.int32).astype(F32)
        spread = jnp.maximum(real * real - square, 1.0)
        raising = jnp.sqrt(jnp.maximum(4.0 * real * real - 1.0, 1.0) / spread)
        previous = real - 1.0
        lowering = jnp.sqrt(
            jnp.maximum(previous * previous - square, 0.0) / jnp.maximum(4.0 * previous * previous - 1.0, 1.0)
        )
        raised = raising * (cosine * latest - lowering * before)
        result = jnp.where(real == order, diagonal, jnp.where(real > order, raised, 0.0))
        value = result * quadrature
        for tile in range(tiles):
            start = pl.multiple_of((tile * degrees + degree) * owned, owned)
            steps_ref[pl.ds(start, owned), :] = value[:, tile * LANES : (tile + 1) * LANES]
        return result, latest

    nothing = order * cosine * 0.0
    lax.fori_loop(0, degrees, advance, (nothing, nothing), unroll=8)
    half = degrees // 2
    for k in range(owned):
        for parity in range(2):
            for tile in range(tiles):
                start = tile * degrees * owned + parity * owned + k
                mine = steps_ref[pl.ds(start, half, stride=2 * owned), :]
                legendre_ref[
                    k, parity * half : (parity + 1) * half, tile * LANES : (tile + 1) * LANES
                ] = mine.astype(BF16)

    twice = (iota((channels, wide), 1) // 2 == iota((channels, wide), 0)).astype(F32).astype(BF16)
    across = (iota((group, wide), 1) % group == iota((group, wide), 0)).astype(F32).astype(BF16)
    shape = (wide, wide)
    row, column = iota(shape, 0), iota(shape, 1)
    row_part, column_part = row % 2, column // channels
    same_group = row // 2 // group == column % channels // group
    straight = row_part == column_part
    sign = jnp.where(row_part > column_part, 1.0, -1.0)

    def expanded(dy, dx):
        doubled = dot_nn(weight_ref[dy, dx], twice).astype(BF16)
        return dot_tn(doubled, across)

    for dy in range(taps):
        tap = [expanded(dy, dx) for dx in range(taps)]
        base_ref[dy, 0] = jnp.where(same_group & straight, tap[radius], 0.0)
        for far in range(1, radius + 1):
            high, low = tap[radius + far], tap[radius - far]
            both = jnp.where(straight, high + low, sign * (high - low))
            base_ref[dy, far] = jnp.where(same_group, both, 0.0)
    same_channel = straight & (row // 2 == column % channels)
    identity = same_channel.astype(F32).astype(BF16)

    def per_order(k, carry):
        factors = [
            jnp.where(straight, turn_ref[2 * far, k], turn_ref[2 * far + 1, k]) for far in range(radius)
        ]
        for dy in range(taps):
            total = base_ref[dy, 0]
            for far in range(radius):
                total = total + base_ref[dy, far + 1] * factors[far]
            mixing_ref[k, :, dy * wide : (dy + 1) * wide] = total.astype(BF16)
        mixing_ref[k, :, taps * wide :] = identity
        return carry

    lax.fori_loop(0, owned, per_order, 0)


def project_kernel(
    radius, field_ref, inner_ref, rim_ref, mixing_ref, legendre_ref, out_ref, rows_ref, plain_ref
):
    members, height, owned, wide = field_ref.shape
    places = members * height
    pad = radius * owned
    batch = out_ref.shape[0]
    step = pl.program_id(0)
    taps = 2 * radius + 1

    @pl.when(step == 0)
    def _():
        rows_ref[:pad, :] = jnp.zeros((pad, rows_ref.shape[1]), F32)
        rows_ref[pad + places * owned :, :] = jnp.zeros((pad, rows_ref.shape[1]), F32)
        for source in range(members):
            for row in range(height):
                start = (source * height + row) * owned
                plain_ref[start : start + owned, :wide] = field_ref[source, row].astype(F32)
                if radius <= row < height - radius:
                    mine = inner_ref[source, row - radius]
                else:
                    mine = rim_ref[source, row if row < radius else row - (height - 2 * radius)]
                rows_ref[pad + start : pad + start + owned, :wide] = mine.astype(F32)

    for at in range(batch):
        k = step * batch + at
        pieces = [rows_ref[pl.ds(dy * owned + k, places, stride=owned), :] for dy in range(taps)]
        pieces.append(plain_ref[pl.ds(k, places, stride=owned), :])
        stacked = jnp.concatenate([piece[:, :wide].astype(BF16) for piece in pieces], axis=1)
        mixed = dot_nt(mixing_ref[at], stacked).astype(BF16)
        found = dot_nt(mixed, legendre_ref[at][:, :places])
        half = found.shape[1] // 2
        out_ref[at, 0] = found[:, :half]
        out_ref[at, 1] = found[:, half:]


def per_device(atmosphere, first_weight, first_bias, second_weight):
    members = lax.axis_size("lat")
    position = lax.axis_index("lat")
    channels, height, length = atmosphere.shape
    group, taps = first_weight.shape[1], first_weight.shape[3]
    radius = taps // 2
    groups = channels // group
    inner = height - 2 * radius
    owned = ORDERS // members
    wide = 2 * channels
    places = height * members

    forward = [(i, i + 1) for i in range(members - 1)]
    backward = [(i + 1, i) for i in range(members - 1)]
    last = atmosphere[:, height - radius :].reshape(channels * radius, length)
    first = atmosphere[:, :radius].reshape(channels * radius, length)
    before = lax.ppermute(last, "lat", forward)
    after = lax.ppermute(first, "lat", backward)

    bias = jnp.broadcast_to(first_bias[:, None], (channels, 128))
    block = height * group
    rim_rows = taps * radius * group
    shapes = jax.ShapeDtypeStruct
    edge, rim, fourier, send_field, send_inner = call(
        lambda *refs: interior_kernel(group, *refs),
        "interior",
        (
            shapes((2 * radius, channels, length), F32),
            shapes((groups * 2 * rim_rows, radius * group), BF16),
            shapes((length, 2 * ORDERS), BF16),
            shapes((members, height, owned, wide), BF16),
            shapes((members, inner, owned, wide), BF16),
        ),
        [
            pltpu.VMEM((groups * taps * block, block), BF16),
            pltpu.VMEM((taps * block, length), F32),
            pltpu.VMEM((inner * channels, length), BF16),
            pltpu.VMEM((2 * height * channels, ORDERS), F32),
        ],
        2 * taps * block * block * length * groups,
        (first_weight.transpose(2, 3, 1, 0), bias, atmosphere.reshape(channels * height, length)),
    )
    got_field = lax.all_to_all(send_field, "lat", 0, 0, tiled=True)
    got_inner = lax.all_to_all(send_inner, "lat", 0, 0, tiled=True)

    send_rim = call(
        lambda *refs: rim_kernel(group, radius, *refs),
        "rim",
        shapes((members, 2 * radius, owned, wide), BF16),
        [
            pltpu.VMEM((rim_rows, length), F32),
            pltpu.VMEM((2 * radius * channels, length), BF16),
        ],
        2 * groups * 2 * rim_rows * radius * group * length,
        (rim, edge, before, after, fourier),
    )
    got_rim = lax.all_to_all(send_rim, "lat", 0, 0, tiled=True)

    angle = (position * owned + 1 + jnp.arange(owned, dtype=jnp.int32)).astype(F32) * (2.0 * math.pi / length)
    turns = jnp.stack([f(far * angle) for far in range(1, radius + 1) for f in (jnp.cos, jnp.sin)])
    colatitude = np.pi * (np.arange(places) + 0.5) / places
    cosine = np.cos(colatitude)
    cosine[places // 2 :] = -cosine[: places // 2][::-1]
    sine = np.sin(np.minimum(colatitude, colatitude[::-1]))
    sphere = np.stack([cosine, np.log(sine), np.pi * sine / np.sqrt(places)]).astype(np.float32)
    spread = -(-places // LANES) * LANES
    sphere = np.pad(sphere, ((0, 0), (0, spread - places)))
    lanes = max(wide, LANES)
    whole = pl.BlockSpec(memory_space=pltpu.VMEM)
    legendre, mixing = call(
        lambda *refs: tables_kernel(group, *refs),
        "tables",
        (
            shapes((owned, DEGREES, spread), BF16),
            shapes((owned, wide, (taps + 1) * wide), BF16),
        ),
        [
            pltpu.VMEM((spread // LANES * DEGREES * owned, LANES), F32),
            pltpu.VMEM((taps, radius + 1, wide, wide), F32),
        ],
        2 * owned * wide * taps * wide * 8,
        (turns, jnp.asarray(sphere), second_weight.transpose(2, 3, 1, 0)),
        in_specs=[pl.BlockSpec(memory_space=pltpu.SMEM), whole, whole],
    )

    batch = math.gcd(owned, 4)
    keep = lambda a: pl.BlockSpec(a.shape, lambda i: (0,) * a.ndim)
    cut = lambda a: pl.BlockSpec((batch,) + a.shape[1:], lambda i: (i,) + (0,) * (a.ndim - 1))
    out_shape = shapes((owned, 2, wide, DEGREES // 2), F32)
    spectrum = call(
        lambda *refs: project_kernel(radius, *refs),
        "project",
        out_shape,
        [
            pltpu.VMEM(((places + 2 * radius) * owned, lanes), F32),
            pltpu.VMEM((places * owned, lanes), F32),
        ],
        2 * owned * wide * places * ((taps + 1) * wide + DEGREES),
        (got_field, got_inner, got_rim, mixing, legendre),
        grid=(owned // batch,),
        in_specs=[keep(got_field), keep(got_inner), keep(got_rim), cut(mixing), cut(legendre)],
        out_specs=cut(out_shape),
    )
    return spectrum.reshape(owned, 2, channels, 2, DEGREES // 2)


def solution(mesh):
    placed = (
        P("chan", "lat", None),
        P("chan", None, None, None),
        P("chan"),
        P("chan", None, None, None),
    )
    return jax.shard_map(
        per_device,
        mesh=mesh,
        in_specs=placed,
        out_specs=P("lat", None, "chan", None, None),
        check_vma=False,
    )
```

```python
import math

import jax
import jax.numpy as jnp
import numpy as np
from jax import lax
from jax.experimental import pallas as pl
from jax.experimental.pallas import tpu as pltpu
from jax.sharding import PartitionSpec as P

ORDERS = 128
DEGREES = 256
LANES = 128
F32 = jnp.float32
BF16 = jnp.bfloat16


def dot_tn(left, right):
    return lax.dot_general(left, right, (((0,), (0,)), ((), ())), preferred_element_type=F32)


def dot_nt(left, right):
    return lax.dot_general(left, right, (((1,), (1,)), ((), ())), preferred_element_type=F32)


def dot_nn(left, right):
    return jnp.dot(left, right, preferred_element_type=F32)


def iota(shape, dim):
    return lax.broadcasted_iota(jnp.int32, shape, dim)


def gelu(value):
    return 0.5 * value * (1.0 + lax.erf(value * math.sqrt(0.5)))


VMEM = pl.BlockSpec(memory_space=pltpu.VMEM)
SMEM = pl.BlockSpec(memory_space=pltpu.SMEM)
HBM = pl.BlockSpec(memory_space=pltpu.HBM)


def bytes_of(arrays):
    return sum(math.prod(a.shape) * a.dtype.itemsize for a in jax.tree.leaves(arrays))


def call(kernel, name, out_shape, scratch, mebibytes, flops, args, in_specs=None, out_specs=None):
    size = bytes_of((args, out_shape))
    return pl.pallas_call(
        kernel,
        out_shape=out_shape,
        in_specs=in_specs or [VMEM] * len(args),
        out_specs=out_specs or jax.tree.map(lambda _: VMEM, out_shape),
        scratch_shapes=scratch,
        compiler_params=pltpu.CompilerParams(vmem_limit_bytes=mebibytes * 2**20),
        cost_estimate=pl.CostEstimate(flops=flops, transcendentals=0, bytes_accessed=size),
        name=name,
    )(*args)


def turned(number, length):
    number = number.astype(F32)
    number = number - length * jnp.floor(number / length)
    return number * (2.0 * math.pi / length)


def write_fourier(fourier_ref, length, orders):
    tile = 128
    factor = 1.0 / math.sqrt(length)
    shape = (tile, orders)
    fine = turned(iota(shape, 0) * (iota(shape, 1) + 1), length)
    fine_cos, fine_sin = jnp.cos(fine), jnp.sin(fine)
    blocks = length // tile
    padded = -(-blocks // 8) * 8
    shape = (padded, orders)
    coarse = turned(iota(shape, 0) * tile * (iota(shape, 1) + 1), length)
    coarse_cos, coarse_sin = jnp.cos(coarse) * factor, jnp.sin(coarse) * factor
    for block in range(blocks):
        cosine = coarse_cos[block : block + 1, :]
        sine = coarse_sin[block : block + 1, :]
        rows = slice(block * tile, (block + 1) * tile)
        fourier_ref[rows, :orders] = (cosine * fine_cos - sine * fine_sin).astype(BF16)
        fourier_ref[rows, orders:] = (-(sine * fine_cos + cosine * fine_sin)).astype(BF16)


def write_spectra(send_ref, slot, real, imaginary):
    members, _, owned, _ = send_ref.shape
    flipped = jnp.concatenate([real, imaginary], axis=0).T
    for device in range(members):
        send_ref[device, slot] = flipped[device * owned : (device + 1) * owned, :].astype(BF16)


def taps_of(weight_ref, dx):
    return jnp.concatenate([weight_ref[dy, dx] for dy in range(weight_ref.shape[0])], axis=0)


def shifted_sum(partial_ref, rows, height, first, count):
    taps = rows // height
    radius = taps // 2
    total = None
    for dx in range(taps):
        start = dx * height + first
        piece = partial_ref[start : start + count, :]
        if dx != radius:
            piece = pltpu.roll(piece, (radius - dx) % piece.shape[1], 1)
        total = piece if total is None else total + piece
    return total


def edges_kernel(group, radius, groups, field_ref, pair_ref, cross_ref):
    block = field_ref.shape[0] // groups
    height = block // group
    depth = radius * group
    parity = lax.axis_index("lat") % 2
    shape = (2 * depth, block)
    place, column = iota(shape, 0), iota(shape, 1)
    far = (place // depth + parity) % 2 == 0
    row = place % radius + jnp.where(far, height - radius, 0)
    chosen = column == place % depth // radius * height + row
    selector = chosen.astype(F32).astype(BF16)
    for g in range(groups):
        found = dot_nn(selector, field_ref[g * block : (g + 1) * block, :]).astype(BF16)
        pair_ref[g * depth : (g + 1) * depth, :] = found[:depth, :]
        cross_ref[g * depth : (g + 1) * depth, :] = found[depth:, :]


def interior_kernel(
    group, weight_ref, bias_ref, field_ref,
    edge_ref, rim_ref, fourier_ref, send_ref,
    band_ref, partial_ref, hidden_ref, spectra_ref,
):
    taps = weight_ref.shape[0]
    radius = taps // 2
    channels = weight_ref.shape[3]
    groups = channels // group
    height = field_ref.shape[0] // channels
    orders = fourier_ref.shape[1] // 2
    inner = height - 2 * radius
    block = height * group
    rows = taps * block

    write_fourier(fourier_ref, field_ref.shape[1], orders)
    shape = (taps * group, height * block)
    place = iota(shape, 0)
    column = iota(shape, 1)
    out_row, column = column // block, column % block
    chosen = (place % group == column // height) & (place // group == column % height - out_row + radius)
    selector = chosen.astype(F32).astype(BF16)
    rim_shape = (taps * group, radius * group)
    rim_place = iota(rim_shape, 0)
    rim_column = iota(rim_shape, 1)
    same = rim_place % group == rim_column // radius
    rim_row = rim_column % radius
    rim_rows = taps * radius * group
    for dx in range(taps):
        mine = taps_of(weight_ref, dx)
        spread = dot_tn(mine, selector).astype(BF16)
        for g in range(groups):
            for row in range(height):
                start = g * rows + dx * block + row * group
                band_ref[start : start + group, :] = spread[
                    g * group : (g + 1) * group, row * block : (row + 1) * block
                ]
        for side in range(2):
            for row in range(radius):
                tap = rim_row - row + (0 if side == 0 else taps - 1)
                pick = (same & (rim_place // group == tap)).astype(F32).astype(BF16)
                spread = dot_tn(mine, pick).astype(BF16)
                for g in range(groups):
                    start = (g * 2 + side) * rim_rows + (dx * radius + row) * group
                    rim_ref[start : start + group, :] = spread[g * group : (g + 1) * group, :]

    def per_group(g, carry):
        band = band_ref[pl.ds(pl.multiple_of(g * rows, 16), rows), :]
        field = field_ref[pl.ds(pl.multiple_of(g * block, 16), block), :]
        partial_ref[...] = dot_nn(band, field)
        mine = pl.ds(pl.multiple_of(g * group, 16), group)
        bias = bias_ref[mine, :][:, :1]
        for row in range(height):
            total = shifted_sum(partial_ref, rows, block, row * group, group) + bias
            if radius <= row < height - radius:
                start = pl.multiple_of((row - radius) * channels + g * group, 16)
                hidden_ref[pl.ds(start, group), :] = gelu(total).astype(BF16)
            else:
                edge_ref[row if row < radius else row - inner, mine, :] = total
        return carry

    lax.fori_loop(0, groups, per_group, 0)

    found = dot_nn(field_ref[...], fourier_ref[...])
    total = height * channels
    for part in range(2):
        spectra_ref[part * total : (part + 1) * total, :] = found[:, part * orders : (part + 1) * orders]
    for row in range(height):
        real, imaginary = (
            spectra_ref[pl.ds(part * total + row, channels, stride=height), :] for part in range(2)
        )
        write_spectra(send_ref, row, real, imaginary)
    found = dot_nn(hidden_ref[...], fourier_ref[...])
    for row in range(inner):
        mine = found[row * channels : (row + 1) * channels, :]
        write_spectra(send_ref, height + row, mine[:, :orders], mine[:, orders:])


def rim_kernel(
    group, radius, rim_ref, edge_ref, pair_ref, cross_ref, fourier_ref, early_ref,
    send_ref, partial_ref, hidden_ref,
):
    channels = edge_ref.shape[1]
    groups = channels // group
    orders = fourier_ref.shape[1] // 2
    rows = partial_ref.shape[0]
    depth = radius * group
    early = early_ref.shape[1]
    position = lax.axis_index("lat")
    parity = position % 2
    polar = (position == 0) | (position == lax.axis_size("lat") - 1)

    def per_group(g, carry):
        for halo_ref, side in ((pair_ref, 1 - parity), (cross_ref, parity)):
            rim = rim_ref[pl.ds(pl.multiple_of((g * 2 + side) * rows, 16), rows), :]
            if halo_ref is cross_ref:
                rim = jnp.where(polar, jnp.zeros_like(rim), rim)
            halo = halo_ref[pl.ds(pl.multiple_of(g * depth, 16), depth), :]
            partial_ref[...] = dot_nn(rim, halo)
            for row in range(radius):
                total = shifted_sum(partial_ref, rows, depth, row * group, group)
                place = side * radius + row
                total = total + edge_ref[place, pl.ds(pl.multiple_of(g * group, 16), group), :]
                start = pl.multiple_of(place * channels + g * group, 16)
                hidden_ref[pl.ds(start, group), :] = gelu(total).astype(BF16)
        return carry

    lax.fori_loop(0, groups, per_group, 0)
    send_ref[:, :early] = early_ref[...]
    found = dot_nn(hidden_ref[...], fourier_ref[...])
    for row in range(2 * radius):
        mine = found[row * channels : (row + 1) * channels, :]
        write_spectra(send_ref, early + row, mine[:, :orders], mine[:, orders:])


def tables_kernel(
    group, turn_ref, sphere_ref, weight_ref,
    table_ref,
    steps_ref, rate_ref, base_ref, turned_ref,
):
    taps = weight_ref.shape[0]
    radius = taps // 2
    channels = weight_ref.shape[3]
    degrees = rate_ref.shape[0] // 2
    owned = table_ref.shape[0]
    wide = 2 * channels
    head = sphere_ref.shape[1]
    places = head * LANES // owned
    first_order = lax.axis_index("lat") * owned + 1

    shape = (degrees, LANES)
    order = (iota(shape, 1) % owned + first_order).astype(F32)
    degree = iota(shape, 0).astype(F32)
    previous = degree - 1.0
    raising = jnp.sqrt(
        jnp.maximum(4.0 * degree * degree - 1.0, 1.0) / jnp.maximum(degree * degree - order * order, 1.0)
    )
    lowering = jnp.sqrt(
        jnp.maximum(previous * previous - order * order, 0.0)
        / jnp.maximum(4.0 * previous * previous - 1.0, 1.0)
    )
    rate_ref[:degrees, :] = raising
    rate_ref[degrees:, :] = lowering

    shape = (ORDERS, LANES)
    number = (iota(shape, 0) + 1).astype(F32)
    ratio = jnp.where(
        iota(shape, 0) < iota(shape, 1) % owned + first_order, jnp.log((2.0 * number - 1.0) / (2.0 * number)), 0.0
    )
    log_ratio = jnp.sum(ratio, axis=0, keepdims=True)
    shape = (head, LANES)
    whole_order = iota(shape, 1) % owned + first_order
    order = whole_order.astype(F32)
    cosine, log_sine, quadrature = sphere_ref[0], sphere_ref[1], sphere_ref[2]
    diagonal = jnp.exp(0.5 * (jnp.log((2.0 * order + 1.0) / 2.0) + log_ratio) + order * log_sine)

    twice = (iota((channels, wide), 1) // 2 == iota((channels, wide), 0)).astype(F32).astype(BF16)
    across = (iota((group, wide), 1) % group == iota((group, wide), 0)).astype(F32).astype(BF16)
    shape = (wide, wide)
    row, column = iota(shape, 0), iota(shape, 1)
    row_part, column_part = row % 2, column // channels
    same_group = row // 2 // group == column % channels // group
    straight = row_part == column_part
    sign = jnp.where(row_part > column_part, 1.0, -1.0)
    flat = jnp.concatenate([weight_ref[dy, dx] for dy in range(taps) for dx in range(taps)], axis=0)
    doubled = dot_nn(flat, twice).astype(BF16)

    def expanded(dy, dx):
        start = (dy * taps + dx) * group
        return dot_tn(doubled[start : start + group, :], across)

    for dy in range(taps):
        tap = [expanded(dy, dx) for dx in range(taps)]
        base_ref[dy, 0] = jnp.where(same_group & straight, tap[radius], 0.0)
        for far in range(1, radius + 1):
            high, low = tap[radius + far], tap[radius - far]
            both = jnp.where(straight, high + low, sign * (high - low))
            base_ref[dy, far] = jnp.where(same_group, both, 0.0)
    steps = degrees // owned

    def per_order(k, carried):
        latest, before = carried
        for step in range(steps):
            at = k * steps + step
            up = jnp.broadcast_to(rate_ref[pl.ds(at, 1), :], (head, LANES))
            down = jnp.broadcast_to(rate_ref[pl.ds(degrees + at, 1), :], (head, LANES))
            raised = up * (cosine * latest - down * before)
            latest, before = jnp.where(whole_order == at, diagonal, raised), latest
            steps_ref[pl.ds(pl.multiple_of(at * head, 8), head), :] = latest * quadrature
        factors = [
            jnp.where(straight, turn_ref[2 * far, k], turn_ref[2 * far + 1, k]) for far in range(radius)
        ]
        for dy in range(taps):
            total = base_ref[dy, 0]
            for far in range(radius):
                total = total + base_ref[dy, far + 1] * factors[far]
            table_ref[k, :wide, dy * wide : (dy + 1) * wide] = total.astype(BF16)
        return latest, before

    nothing = order * cosine * 0.0
    lax.fori_loop(0, owned, per_order, (nothing, nothing))
    half = degrees // 2
    total = head * LANES
    for parity in range(2):
        for at in range(head):
            mine = steps_ref[pl.ds(parity * head + at, half, stride=2 * head), :]
            turned_ref[parity * total + at * LANES : parity * total + (at + 1) * LANES, :] = mine.T
    for parity in range(2):
        for k in range(owned):
            mine = turned_ref[pl.ds(parity * total + k, places, stride=owned), :]
            rows = slice(parity * places, (parity + 1) * places)
            table_ref[k, rows, taps * wide :] = mine.astype(BF16)


def project_kernel(
    radius, got_ref, table_ref, out_hbm, rows_ref, plain_ref, out_ref, semaphores
):
    members, height, owned, wide = got_ref.shape
    height = height // 2
    places = members * height
    pad = radius * owned
    taps = 2 * radius + 1
    slots = out_ref.shape[0]

    rows_ref[:pad, :] = jnp.zeros((pad, rows_ref.shape[1]), F32)
    rows_ref[pad + places * owned :, :] = jnp.zeros((pad, rows_ref.shape[1]), F32)
    for source in range(members):
        for row in range(height):
            start = (source * height + row) * owned
            plain_ref[start : start + owned, :wide] = got_ref[source, row].astype(F32)
            if radius <= row < height - radius:
                place = height + row - radius
            elif row < radius:
                place = 2 * height - 2 * radius + row
            else:
                place = height + row
            rows_ref[pad + start : pad + start + owned, :wide] = got_ref[source, place].astype(F32)

    row, column = iota((wide, wide), 0), iota((wide, wide), 1)
    identity = (column == row % 2 * (wide // 2) + row // 2).astype(F32).astype(BF16)

    def sent(k, slot):
        return pltpu.make_async_copy(out_ref.at[slot], out_hbm.at[k], semaphores.at[slot])

    for k in range(owned):
        slot = k % slots
        pieces = [rows_ref[pl.ds(dy * owned + k, places, stride=owned), :] for dy in range(taps)]
        pieces.append(plain_ref[pl.ds(k, places, stride=owned), :])
        stacked = jnp.concatenate([piece[:, :wide].astype(BF16) for piece in pieces], axis=1)
        mixing = jnp.concatenate([table_ref[k, :wide, : taps * wide], identity], axis=1)
        mixed = dot_nt(mixing, stacked).astype(BF16)
        if k >= slots:
            sent(k - slots, slot).wait()
        for parity in range(2):
            rows = slice(parity * places, (parity + 1) * places)
            out_ref[slot, parity] = dot_nn(mixed, table_ref[k, rows, taps * wide :])
        sent(k, slot).start()
    for k in range(max(0, owned - slots), owned):
        sent(k, k % slots).wait()


def per_device(atmosphere, first_weight, first_bias, second_weight):
    members = lax.axis_size("lat")
    position = lax.axis_index("lat")
    channels, height, length = atmosphere.shape
    group, taps = first_weight.shape[1], first_weight.shape[3]
    radius = taps // 2
    groups = channels // group
    inner = height - 2 * radius
    owned = ORDERS // members
    wide = 2 * channels
    places = height * members

    shapes = jax.ShapeDtypeStruct
    block = height * group
    rim_rows = taps * radius * group
    first_taps = first_weight.transpose(2, 3, 1, 0)
    second_taps = second_weight.transpose(2, 3, 1, 0)
    flat = atmosphere.reshape(channels * height, length)
    pair, cross = call(
        lambda *refs: edges_kernel(group, radius, groups, *refs),
        "edges",
        (shapes((channels * radius, length), BF16), shapes((channels * radius, length), BF16)),
        [],
        8,
        4 * radius * channels * block * length,
        (flat,),
    )
    pairs = [(i, i ^ 1) for i in range(members) if i ^ 1 < members]
    crosses = [(i, (i + 1 if i % 2 else i - 1) % members) for i in range(members)]
    cross = lax.ppermute(cross, "lat", crosses)
    pair = lax.ppermute(pair, "lat", pairs)

    bias = jnp.broadcast_to(first_bias[:, None], (channels, LANES))
    edge, rim, fourier, early = call(
        lambda *refs: interior_kernel(group, *refs),
        "interior",
        (
            shapes((2 * radius, channels, length), F32),
            shapes((groups * 2 * rim_rows, radius * group), BF16),
            shapes((length, 2 * ORDERS), BF16),
            shapes((members, height + inner, owned, wide), BF16),
        ),
        [
            pltpu.VMEM((groups * taps * block, block), BF16),
            pltpu.VMEM((taps * block, length), F32),
            pltpu.VMEM((inner * channels, length), BF16),
            pltpu.VMEM((2 * height * channels, ORDERS), F32),
        ],
        10,
        2 * taps * block * block * length * groups,
        (first_taps, bias, flat),
    )
    send = call(
        lambda *refs: rim_kernel(group, radius, *refs),
        "rim",
        shapes((members, 2 * height, owned, wide), BF16),
        [
            pltpu.VMEM((rim_rows, length), F32),
            pltpu.VMEM((2 * radius * channels, length), BF16),
        ],
        6,
        2 * groups * 2 * rim_rows * radius * group * length,
        (rim, edge, pair, cross, fourier, early),
    )
    got = lax.all_to_all(send, "lat", 0, 0, tiled=True)

    angle = (position * owned + 1 + jnp.arange(owned, dtype=jnp.int32)).astype(F32) * (2.0 * math.pi / length)
    turns = jnp.stack([f(far * angle) for far in range(1, radius + 1) for f in (jnp.cos, jnp.sin)])
    colatitude = np.pi * (np.arange(places) + 0.5) / places
    cosine = np.cos(colatitude)
    cosine[places // 2 :] = -cosine[: places // 2][::-1]
    sine = np.sin(np.minimum(colatitude, colatitude[::-1]))
    sphere = np.stack([cosine, np.log(sine), np.pi * sine / np.sqrt(places)]).astype(np.float32)
    head = places * owned // LANES
    sphere = np.repeat(sphere.reshape(3, head, LANES // owned), owned, axis=2)
    table = call(
        lambda *refs: tables_kernel(group, *refs),
        "tables",
        shapes((owned, max(wide, 2 * places), taps * wide + DEGREES // 2), BF16),
        [
            pltpu.VMEM((DEGREES * head, LANES), F32),
            pltpu.VMEM((2 * DEGREES, LANES), F32),
            pltpu.VMEM((taps, radius + 1, wide, wide), F32),
            pltpu.VMEM((2 * head * LANES, DEGREES // 2), F32),
        ],
        6,
        2 * owned * wide * taps * wide * 8,
        (turns, jnp.asarray(sphere), second_taps),
        in_specs=[SMEM, VMEM, VMEM],
    )

    lanes = max(wide, LANES)
    slots = owned
    spectrum = call(
        lambda *refs: project_kernel(radius, *refs),
        "project",
        shapes((owned, 2, wide, DEGREES // 2), F32),
        [
            pltpu.VMEM(((places + 2 * radius) * owned, lanes), F32),
            pltpu.VMEM((places * owned, lanes), F32),
            pltpu.VMEM((slots, 2, wide, DEGREES // 2), F32),
            pltpu.SemaphoreType.DMA((slots,)),
        ],
        6,
        2 * owned * wide * places * ((taps + 1) * wide + DEGREES),
        (got, table),
        out_specs=HBM,
    )
    return spectrum.reshape(owned, 2, channels, 2, DEGREES // 2)


def solution(mesh):
    placed = (
        P("chan", "lat", None),
        P("chan", None, None, None),
        P("chan"),
        P("chan", None, None, None),
    )
    return jax.shard_map(
        per_device,
        mesh=mesh,
        in_specs=placed,
        out_specs=P("lat", None, "chan", None, None),
        check_vma=False,
    )
```

```python
import math

import jax
import jax.numpy as jnp
import numpy as np
from jax import lax
from jax.experimental import pallas as pl
from jax.experimental.pallas import tpu as pltpu
from jax.sharding import PartitionSpec as P

ORDERS = 128
DEGREES = 256
LANES = 128
F32 = jnp.float32
BF16 = jnp.bfloat16


def dot_tn(left, right):
    return lax.dot_general(left, right, (((0,), (0,)), ((), ())), preferred_element_type=F32)


def dot_nt(left, right):
    return lax.dot_general(left, right, (((1,), (1,)), ((), ())), preferred_element_type=F32)


def dot_nn(left, right):
    return jnp.dot(left, right, preferred_element_type=F32)


def iota(shape, dim):
    return lax.broadcasted_iota(jnp.int32, shape, dim)


def gelu(value):
    return 0.5 * value * (1.0 + lax.erf(value * math.sqrt(0.5)))


VMEM = pl.BlockSpec(memory_space=pltpu.VMEM)
SMEM = pl.BlockSpec(memory_space=pltpu.SMEM)
HBM = pl.BlockSpec(memory_space=pltpu.HBM)


def bytes_of(arrays):
    return sum(math.prod(a.shape) * a.dtype.itemsize for a in jax.tree.leaves(arrays))


def call(kernel, name, out_shape, scratch, mebibytes, flops, args, in_specs=None, out_specs=None):
    size = bytes_of((args, out_shape))
    return pl.pallas_call(
        kernel,
        out_shape=out_shape,
        in_specs=in_specs or [VMEM] * len(args),
        out_specs=out_specs or jax.tree.map(lambda _: VMEM, out_shape),
        scratch_shapes=scratch,
        compiler_params=pltpu.CompilerParams(vmem_limit_bytes=mebibytes * 2**20),
        cost_estimate=pl.CostEstimate(flops=flops, transcendentals=0, bytes_accessed=size),
        name=name,
    )(*args)


def turned(number, length):
    number = number.astype(F32)
    number = number - length * jnp.floor(number / length)
    return number * (2.0 * math.pi / length)


def write_fourier(fourier_ref, length, orders):
    tile = 128
    factor = 1.0 / math.sqrt(length)
    shape = (tile, orders)
    fine = turned(iota(shape, 0) * (iota(shape, 1) + 1), length)
    fine_cos, fine_sin = jnp.cos(fine), jnp.sin(fine)
    blocks = length // tile
    padded = -(-blocks // 8) * 8
    shape = (padded, orders)
    coarse = turned(iota(shape, 0) * tile * (iota(shape, 1) + 1), length)
    coarse_cos, coarse_sin = jnp.cos(coarse) * factor, jnp.sin(coarse) * factor
    for block in range(blocks):
        cosine = coarse_cos[block : block + 1, :]
        sine = coarse_sin[block : block + 1, :]
        rows = slice(block * tile, (block + 1) * tile)
        fourier_ref[rows, :orders] = (cosine * fine_cos - sine * fine_sin).astype(BF16)
        fourier_ref[rows, orders:] = (-(sine * fine_cos + cosine * fine_sin)).astype(BF16)


def write_spectra(send_ref, slot, real, imaginary):
    members, _, owned, _ = send_ref.shape
    flipped = jnp.concatenate([real, imaginary], axis=0).T
    for device in range(members):
        send_ref[device, slot] = flipped[device * owned : (device + 1) * owned, :].astype(BF16)


def taps_of(weight_ref, dx):
    return jnp.concatenate([weight_ref[dy, dx] for dy in range(weight_ref.shape[0])], axis=0)


def shifted_sum(partial_ref, rows, height, first, count):
    taps = rows // height
    radius = taps // 2
    total = None
    for dx in range(taps):
        start = dx * height + first
        piece = partial_ref[start : start + count, :]
        if dx != radius:
            piece = pltpu.roll(piece, (radius - dx) % piece.shape[1], 1)
        total = piece if total is None else total + piece
    return total


def picked(group, radius, groups, field_ref, crossing):
    block = field_ref.shape[0] // groups
    height = block // group
    depth = radius * group
    shape = (depth, block)
    place, column = iota(shape, 0), iota(shape, 1)
    far = (lax.axis_index("lat") + crossing) % 2 == 0
    row = place % radius + jnp.where(far, height - radius, 0)
    chosen = column == place // radius * height + row
    selector = chosen.astype(F32).astype(BF16)
    for g in range(groups):
        yield dot_nn(selector, field_ref[g * block : (g + 1) * block, :]).astype(BF16)


def cross_kernel(group, radius, groups, field_ref, kept_ref, *cross_refs):
    share = groups // len(cross_refs)
    depth = radius * group
    for g, rows in enumerate(picked(group, radius, groups, field_ref, 1)):
        start = g % share * depth
        cross_refs[g // share][start : start + depth, :] = rows
    kept_ref[...] = field_ref[...]


def pair_kernel(group, radius, groups, field_ref, pair_ref):
    depth = radius * group
    for g, rows in enumerate(picked(group, radius, groups, field_ref, 0)):
        pair_ref[g * depth : (g + 1) * depth, :] = rows


def interior_kernel(
    group, weight_ref, bias_ref, field_ref,
    edge_ref, rim_ref, fourier_ref, send_ref,
    band_ref, partial_ref, hidden_ref, spectra_ref, column_ref,
):
    taps = weight_ref.shape[0]
    radius = taps // 2
    channels = weight_ref.shape[3]
    groups = channels // group
    height = field_ref.shape[0] // channels
    orders = fourier_ref.shape[1] // 2
    inner = height - 2 * radius
    block = height * group
    rows = taps * block

    write_fourier(fourier_ref, field_ref.shape[1], orders)
    shape = (channels, channels)
    bias = jnp.where(iota(shape, 0) == iota(shape, 1), bias_ref[...], 0.0)
    column_ref[...] = jnp.broadcast_to(jnp.sum(bias, axis=1, keepdims=True), column_ref.shape)
    shape = (taps * group, height * block)
    place = iota(shape, 0)
    column = iota(shape, 1)
    out_row, column = column // block, column % block
    chosen = (place % group == column // height) & (place // group == column % height - out_row + radius)
    selector = chosen.astype(F32).astype(BF16)
    position = lax.axis_index("lat")
    parity = position % 2
    polar = (position == 0) | (position == lax.axis_size("lat") - 1)
    open_side = jnp.where(polar, 0.0, 1.0)
    depth = radius * group
    rim_shape = (taps * group, 2 * depth)
    rim_place = iota(rim_shape, 0)
    rim_column = iota(rim_shape, 1)
    same = rim_place % group == rim_column % depth // radius
    rim_row = rim_column % radius
    rim_rows = taps * radius * group
    for dx in range(taps):
        mine = taps_of(weight_ref, dx)
        spread = dot_tn(mine, selector).astype(BF16)
        for g in range(groups):
            for row in range(height):
                start = g * rows + dx * block + row * group
                band_ref[start : start + group, :] = spread[
                    g * group : (g + 1) * group, row * block : (row + 1) * block
                ]
        for which in range(2):
            side = 1 - parity if which == 0 else parity
            for row in range(radius):
                tap = rim_row - row + side * (taps - 1)
                own = same & (rim_column // depth == which) & (rim_place // group == tap)
                pick = jnp.where(own, 1.0 if which == 0 else open_side, 0.0)
                spread = dot_tn(mine, pick.astype(BF16)).astype(BF16)
                for g in range(groups):
                    start = (g * 2 + which) * rim_rows + (dx * radius + row) * group
                    rim_ref[start : start + group, :] = spread[g * group : (g + 1) * group, :]

    def per_group(g, carry):
        band = band_ref[pl.ds(pl.multiple_of(g * rows, 16), rows), :]
        field = field_ref[pl.ds(pl.multiple_of(g * block, 16), block), :]
        partial_ref[...] = dot_nn(band, field)
        mine = pl.ds(pl.multiple_of(g * group, 16), group)
        bias = column_ref[mine, :][:, :1]
        for row in range(height):
            total = shifted_sum(partial_ref, rows, block, row * group, group) + bias
            if radius <= row < height - radius:
                start = pl.multiple_of((row - radius) * channels + g * group, 16)
                hidden_ref[pl.ds(start, group), :] = gelu(total).astype(BF16)
            else:
                edge_ref[row if row < radius else row - inner, mine, :] = total
        return carry

    lax.fori_loop(0, groups, per_group, 0)

    found = dot_nn(field_ref[...], fourier_ref[...])
    pitch = height + 1
    total = pitch * channels
    for part in range(2):
        for channel in range(channels):
            start = part * total + channel * pitch
            spectra_ref[start : start + height, :] = found[
                channel * height : (channel + 1) * height, part * orders : (part + 1) * orders
            ]
    for row in range(height):
        real, imaginary = (
            spectra_ref[pl.ds(part * total + row, channels, stride=pitch), :] for part in range(2)
        )
        write_spectra(send_ref, row, real, imaginary)
    found = dot_nn(hidden_ref[...], fourier_ref[...])
    for row in range(inner):
        mine = found[row * channels : (row + 1) * channels, :]
        write_spectra(send_ref, height + row, mine[:, :orders], mine[:, orders:])


def write_rim(group, radius, groups, rim_ref, edge_ref, pair_ref, cross_ref, partial_ref, store):
    rows = partial_ref.shape[0]
    depth = radius * group
    parity = lax.axis_index("lat") % 2

    def per_group(at, carry):
        g = groups[0] + at
        rim = rim_ref[pl.ds(pl.multiple_of(g * rows, 16), rows), :]
        pair = pair_ref[pl.ds(pl.multiple_of(g * depth, 16), depth), :]
        cross = cross_ref[pl.ds(pl.multiple_of(at * depth, 16), depth), :]
        partial_ref[...] = dot_nn(rim, jnp.concatenate([pair, cross], axis=0))
        for which, side in ((0, 1 - parity), (1, parity)):
            mine_ref = partial_ref.at[which * rows // 2 : (which + 1) * rows // 2]
            for row in range(radius):
                total = shifted_sum(mine_ref, rows // 2, depth, row * group, group)
                place = side * radius + row
                total = total + edge_ref[place, pl.ds(pl.multiple_of(g * group, 16), group), :]
                store(place, g, at, gelu(total).astype(BF16))
        return carry

    lax.fori_loop(0, groups[1] - groups[0], per_group, 0)


def first_rim_kernel(group, radius, groups, rim_ref, edge_ref, pair_ref, cross_ref, hidden_ref, partial_ref):
    def store(place, g, at, value):
        hidden_ref[place, pl.ds(pl.multiple_of(at * group, 16), group), :] = value

    write_rim(group, radius, groups, rim_ref, edge_ref, pair_ref, cross_ref, partial_ref, store)


def last_rim_kernel(
    group, radius, groups, rim_ref, edge_ref, pair_ref, cross_ref, fourier_ref, early_ref, *refs
):
    before_refs, (send_hbm, partial_ref, hidden_ref, late_ref, semaphores) = refs[:-5], refs[-5:]
    channels = edge_ref.shape[1]
    orders = fourier_ref.shape[1] // 2
    early = early_ref.shape[1]
    first = pltpu.make_async_copy(early_ref, send_hbm.at[:, pl.ds(0, early)], semaphores.at[0])
    first.start()
    for place in range(2 * radius):
        for before_ref in before_refs:
            size = before_ref.shape[1]
            hidden_ref[place * channels : place * channels + size, :] = before_ref[place]

    def store(place, g, at, value):
        start = pl.multiple_of(place * channels + g * group, 16)
        hidden_ref[pl.ds(start, group), :] = value

    write_rim(group, radius, groups, rim_ref, edge_ref, pair_ref, cross_ref, partial_ref, store)
    found = dot_nn(hidden_ref[...], fourier_ref[...])
    for row in range(2 * radius):
        mine = found[row * channels : (row + 1) * channels, :]
        write_spectra(late_ref, row, mine[:, :orders], mine[:, orders:])
    last = pltpu.make_async_copy(late_ref, send_hbm.at[:, pl.ds(early, 2 * radius)], semaphores.at[1])
    last.start()
    first.wait()
    last.wait()


def tables_kernel(
    group, turn_ref, sphere_ref, weight_ref,
    table_ref,
    steps_ref, rate_ref, base_ref, turned_ref,
):
    taps = weight_ref.shape[0]
    radius = taps // 2
    channels = weight_ref.shape[3]
    degrees = rate_ref.shape[0] // 2
    owned = table_ref.shape[0]
    wide = 2 * channels
    head = sphere_ref.shape[1]
    places = head * LANES // owned
    first_order = lax.axis_index("lat") * owned + 1

    shape = (degrees, LANES)
    order = (iota(shape, 1) % owned + first_order).astype(F32)
    degree = iota(shape, 0).astype(F32)
    previous = degree - 1.0
    raising = jnp.sqrt(
        jnp.maximum(4.0 * degree * degree - 1.0, 1.0) / jnp.maximum(degree * degree - order * order, 1.0)
    )
    lowering = jnp.sqrt(
        jnp.maximum(previous * previous - order * order, 0.0)
        / jnp.maximum(4.0 * previous * previous - 1.0, 1.0)
    )
    rate_ref[:degrees, :] = raising
    rate_ref[degrees:, :] = lowering

    shape = (ORDERS, LANES)
    number = (iota(shape, 0) + 1).astype(F32)
    ratio = jnp.where(
        iota(shape, 0) < iota(shape, 1) % owned + first_order, jnp.log((2.0 * number - 1.0) / (2.0 * number)), 0.0
    )
    log_ratio = jnp.sum(ratio, axis=0, keepdims=True)
    shape = (head, LANES)
    whole_order = iota(shape, 1) % owned + first_order
    order = whole_order.astype(F32)
    cosine, log_sine, quadrature = sphere_ref[0], sphere_ref[1], sphere_ref[2]
    diagonal = jnp.exp(0.5 * (jnp.log((2.0 * order + 1.0) / 2.0) + log_ratio) + order * log_sine)

    twice = (iota((channels, wide), 1) // 2 == iota((channels, wide), 0)).astype(F32).astype(BF16)
    across = (iota((group, wide), 1) % group == iota((group, wide), 0)).astype(F32).astype(BF16)
    shape = (wide, wide)
    row, column = iota(shape, 0), iota(shape, 1)
    row_part, column_part = row // channels, column % 2
    same_group = row % channels // group == column // 2 // group
    straight = row_part == column_part
    sign = jnp.where(column_part > row_part, 1.0, -1.0)
    flat = jnp.concatenate([weight_ref[dy, dx] for dy in range(taps) for dx in range(taps)], axis=0)
    doubled = dot_nn(flat, twice).astype(BF16)

    def expanded(dy, dx):
        start = (dy * taps + dx) * group
        return dot_tn(across, doubled[start : start + group, :])

    for dy in range(taps):
        tap = [expanded(dy, dx) for dx in range(taps)]
        base_ref[dy, 0] = jnp.where(same_group & straight, tap[radius], 0.0)
        for far in range(1, radius + 1):
            high, low = tap[radius + far], tap[radius - far]
            both = jnp.where(straight, high + low, sign * (high - low))
            base_ref[dy, far] = jnp.where(same_group, both, 0.0)
    steps = degrees // owned

    def per_order(k, carried):
        latest, before = carried
        for step in range(steps):
            at = k * steps + step
            up = jnp.broadcast_to(rate_ref[pl.ds(at, 1), :], (head, LANES))
            down = jnp.broadcast_to(rate_ref[pl.ds(degrees + at, 1), :], (head, LANES))
            raised = up * (cosine * latest - down * before)
            latest, before = jnp.where(whole_order == at, diagonal, raised), latest
            steps_ref[pl.ds(pl.multiple_of(at * head, 8), head), :] = latest * quadrature
        factors = [
            jnp.where(straight, turn_ref[2 * far, k], turn_ref[2 * far + 1, k]) for far in range(radius)
        ]
        for dy in range(taps):
            total = base_ref[dy, 0]
            for far in range(radius):
                total = total + base_ref[dy, far + 1] * factors[far]
            table_ref[k, dy * wide : (dy + 1) * wide, :wide] = total.astype(BF16)
        return latest, before

    nothing = order * cosine * 0.0
    lax.fori_loop(0, owned, per_order, (nothing, nothing))
    half = degrees // 2
    total = head * LANES
    for parity in range(2):
        for at in range(head):
            mine = steps_ref[pl.ds(parity * head + at, half, stride=2 * head), :]
            turned_ref[parity * total + at * LANES : parity * total + (at + 1) * LANES, :] = mine.T
    for parity in range(2):
        for k in range(owned):
            mine = turned_ref[pl.ds(parity * total + k, places, stride=owned), :]
            start = taps * wide + parity * places
            table_ref[k, start : start + places, :half] = mine.astype(BF16)


def project_kernel(
    radius, got_ref, table_ref, out_hbm, rows_ref, plain_ref, out_ref, semaphores
):
    members, height, owned, wide = got_ref.shape
    height = height // 2
    places = members * height
    pitch = owned + 1
    pad = radius * pitch
    taps = 2 * radius + 1

    rows_ref[:pad, :] = jnp.zeros((pad, rows_ref.shape[1]), F32)
    rows_ref[pad + places * pitch :, :] = jnp.zeros((pad, rows_ref.shape[1]), F32)
    for source in range(members):
        for row in range(height):
            start = (source * height + row) * pitch
            plain_ref[start : start + owned, :wide] = got_ref[source, row].astype(F32)
            if radius <= row < height - radius:
                place = height + row - radius
            elif row < radius:
                place = 2 * height - 2 * radius + row
            else:
                place = height + row
            rows_ref[pad + start : pad + start + owned, :wide] = got_ref[source, place].astype(F32)

    row, column = iota((wide, wide), 0), iota((wide, wide), 1)
    identity = (row == column % 2 * (wide // 2) + column // 2).astype(F32).astype(BF16)
    identity = jnp.concatenate([identity] * (2 if owned % 2 == 0 else 1), axis=1)
    mix = taps * wide
    half = out_ref.shape[3]

    def sent(k):
        return pltpu.make_async_copy(out_ref.at[k], out_hbm.at[k], semaphores.at[k])

    def gathered(k):
        pieces = [rows_ref[pl.ds(dy * pitch + k, places, stride=pitch), :] for dy in range(taps)]
        pieces.append(plain_ref[pl.ds(k, places, stride=pitch), :])
        return jnp.concatenate([piece[:, :wide].astype(BF16) for piece in pieces], axis=1)

    together = 2 if owned % 2 == 0 else 1
    for first in range(0, owned, together):
        orders = range(first, first + together)
        stacked = jnp.concatenate([gathered(k) for k in orders], axis=0)
        mixing = jnp.concatenate([table_ref[k, :mix, :wide] for k in orders], axis=1)
        mixing = jnp.concatenate([mixing, identity], axis=0)
        both = dot_nn(stacked, mixing)
        for at, k in enumerate(orders):
            mixed = both[at * places : (at + 1) * places, at * wide : (at + 1) * wide].T.astype(BF16)
            legendre = jnp.concatenate(
                [table_ref[k, mix + q * places : mix + (q + 1) * places, :half] for q in range(2)], axis=1
            )
            found = dot_nn(mixed, legendre)
            out_ref[k, 0] = found[:, :half]
            out_ref[k, 1] = found[:, half:]
            sent(k).start()
    for k in range(owned):
        sent(k).wait()


def per_device(atmosphere, first_weight, first_bias, second_weight):
    members = lax.axis_size("lat")
    position = lax.axis_index("lat")
    channels, height, length = atmosphere.shape
    group, taps = first_weight.shape[1], first_weight.shape[3]
    radius = taps // 2
    groups = channels // group
    inner = height - 2 * radius
    owned = ORDERS // members
    wide = 2 * channels
    places = height * members

    shapes = jax.ShapeDtypeStruct
    block = height * group
    rim_rows = taps * radius * group
    first_taps = first_weight.transpose(2, 3, 1, 0)
    second_taps = second_weight.transpose(2, 3, 1, 0)
    flat = atmosphere.reshape(channels * height, length)
    shares = 2 if groups % 2 == 0 else 1
    share = groups // shares
    part = shapes((share * group * radius, length), BF16)
    flat, *crossed = call(
        lambda *refs: cross_kernel(group, radius, groups, *refs),
        "cross_rows",
        (shapes(flat.shape, BF16),) + (part,) * shares,
        [],
        6,
        2 * radius * channels * block * length,
        (flat,),
    )
    crosses = [(i, (i + 1 if i % 2 else i - 1) % members) for i in range(members)]
    crossed = [lax.ppermute(cross, "lat", crosses) for cross in crossed]
    pair = call(
        lambda *refs: pair_kernel(group, radius, groups, *refs),
        "pair_rows",
        shapes((channels * radius, length), BF16),
        [],
        6,
        2 * radius * channels * block * length,
        (flat,),
    )
    pairs = [(i, i ^ 1) for i in range(members) if i ^ 1 < members]
    pair = lax.ppermute(pair, "lat", pairs)

    edge, rim, fourier, early = call(
        lambda *refs: interior_kernel(group, *refs),
        "interior",
        (
            shapes((2 * radius, channels, length), F32),
            shapes((groups * 2 * rim_rows, 2 * radius * group), BF16),
            shapes((length, 2 * ORDERS), BF16),
            shapes((members, height + inner, owned, wide), BF16),
        ),
        [
            pltpu.VMEM((groups * taps * block, block), BF16),
            pltpu.VMEM((taps * block, length), F32),
            pltpu.VMEM((inner * channels, length), BF16),
            pltpu.VMEM((2 * (height + 1) * channels, ORDERS), F32),
            pltpu.VMEM((channels, LANES), F32),
        ],
        10,
        2 * taps * block * block * length * groups,
        (first_taps, first_bias[None, :], flat),
    )
    partial = pltpu.VMEM((2 * rim_rows, length), F32)
    flops = 8 * rim_rows * radius * group * length * share
    before = [
        call(
            lambda *refs: first_rim_kernel(group, radius, (0, share), *refs),
            "rim_first",
            shapes((2 * radius, share * group, length), BF16),
            [partial],
            6,
            flops,
            (rim, edge, pair, cross),
        )
        for cross in crossed[:-1]
    ]
    send = call(
        lambda *refs: last_rim_kernel(group, radius, (groups - share, groups), *refs),
        "rim_last",
        shapes((members, 2 * height, owned, wide), BF16),
        [
            partial,
            pltpu.VMEM((2 * radius * channels, length), BF16),
            pltpu.VMEM((members, 2 * radius, owned, wide), BF16),
            pltpu.SemaphoreType.DMA((2,)),
        ],
        8,
        flops,
        (rim, edge, pair, crossed[-1], fourier, early, *before),
        out_specs=HBM,
    )
    got = lax.all_to_all(send, "lat", 0, 0, tiled=True)

    angle = (position * owned + 1 + jnp.arange(owned, dtype=jnp.int32)).astype(F32) * (2.0 * math.pi / length)
    turns = jnp.stack([f(far * angle) for far in range(1, radius + 1) for f in (jnp.cos, jnp.sin)])
    colatitude = np.pi * (np.arange(places) + 0.5) / places
    cosine = np.cos(colatitude)
    cosine[places // 2 :] = -cosine[: places // 2][::-1]
    sine = np.sin(np.minimum(colatitude, colatitude[::-1]))
    sphere = np.stack([cosine, np.log(sine), np.pi * sine / np.sqrt(places)]).astype(np.float32)
    head = places * owned // LANES
    sphere = np.repeat(sphere.reshape(3, head, LANES // owned), owned, axis=2)
    table = call(
        lambda *refs: tables_kernel(group, *refs),
        "tables",
        shapes((owned, taps * wide + 2 * places, max(wide, DEGREES // 2)), BF16),
        [
            pltpu.VMEM((DEGREES * head, LANES), F32),
            pltpu.VMEM((2 * DEGREES, LANES), F32),
            pltpu.VMEM((taps, radius + 1, wide, wide), F32),
            pltpu.VMEM((2 * head * LANES, DEGREES // 2), F32),
        ],
        6,
        2 * owned * wide * taps * wide * 8,
        (turns, jnp.asarray(sphere), second_taps),
        in_specs=[SMEM, VMEM, VMEM],
    )

    lanes = max(wide, LANES)
    spectrum = call(
        lambda *refs: project_kernel(radius, *refs),
        "project",
        shapes((owned, 2, wide, DEGREES // 2), F32),
        [
            pltpu.VMEM(((places + 2 * radius) * (owned + 1), lanes), F32),
            pltpu.VMEM((places * (owned + 1), lanes), F32),
            pltpu.VMEM((owned, 2, wide, DEGREES // 2), F32),
            pltpu.SemaphoreType.DMA((owned,)),
        ],
        6,
        2 * owned * wide * places * ((taps + 1) * wide + DEGREES),
        (got, table),
        out_specs=HBM,
    )
    return spectrum.reshape(owned, 2, channels, 2, DEGREES // 2)


def solution(mesh):
    placed = (
        P("chan", "lat", None),
        P("chan", None, None, None),
        P("chan"),
        P("chan", None, None, None),
    )
    return jax.shard_map(
        per_device,
        mesh=mesh,
        in_specs=placed,
        out_specs=P("lat", None, "chan", None, None),
        check_vma=False,
    )
```

```python
import math

import jax
import jax.numpy as jnp
import numpy as np
from jax import lax
from jax.experimental import pallas as pl
from jax.experimental.pallas import tpu as pltpu
from jax.sharding import PartitionSpec as P

ORDERS = 128
DEGREES = 256
LANES = 128
F32 = jnp.float32
BF16 = jnp.bfloat16


def dot_tn(left, right):
    return lax.dot_general(left, right, (((0,), (0,)), ((), ())), preferred_element_type=F32)


def dot_nt(left, right):
    return lax.dot_general(left, right, (((1,), (1,)), ((), ())), preferred_element_type=F32)


def dot_nn(left, right):
    return jnp.dot(left, right, preferred_element_type=F32)


def iota(shape, dim):
    return lax.broadcasted_iota(jnp.int32, shape, dim)


def gelu(value):
    return 0.5 * value * (1.0 + lax.erf(value * math.sqrt(0.5)))


VMEM = pl.BlockSpec(memory_space=pltpu.VMEM)
SMEM = pl.BlockSpec(memory_space=pltpu.SMEM)
HBM = pl.BlockSpec(memory_space=pltpu.HBM)


def bytes_of(arrays):
    return sum(math.prod(a.shape) * a.dtype.itemsize for a in jax.tree.leaves(arrays))


def call(kernel, name, out_shape, scratch, mebibytes, flops, args, in_specs=None, out_specs=None):
    size = bytes_of((args, out_shape))
    return pl.pallas_call(
        kernel,
        out_shape=out_shape,
        in_specs=in_specs or [VMEM] * len(args),
        out_specs=out_specs or jax.tree.map(lambda _: VMEM, out_shape),
        scratch_shapes=scratch,
        compiler_params=pltpu.CompilerParams(vmem_limit_bytes=mebibytes * 2**20),
        cost_estimate=pl.CostEstimate(flops=flops, transcendentals=0, bytes_accessed=size),
        name=name,
    )(*args)


def turned(number, length):
    number = number.astype(F32)
    number = number - length * jnp.floor(number / length)
    return number * (2.0 * math.pi / length)


def write_fourier(fourier_ref, length, orders):
    tile = 128
    factor = 1.0 / math.sqrt(length)
    shape = (tile, orders)
    fine = turned(iota(shape, 0) * (iota(shape, 1) + 1), length)
    fine_cos, fine_sin = jnp.cos(fine), jnp.sin(fine)
    blocks = length // tile
    padded = -(-blocks // 8) * 8
    shape = (padded, orders)
    coarse = turned(iota(shape, 0) * tile * (iota(shape, 1) + 1), length)
    coarse_cos, coarse_sin = jnp.cos(coarse) * factor, jnp.sin(coarse) * factor
    for block in range(blocks):
        cosine = coarse_cos[block : block + 1, :]
        sine = coarse_sin[block : block + 1, :]
        rows = slice(block * tile, (block + 1) * tile)
        fourier_ref[rows, :orders] = (cosine * fine_cos - sine * fine_sin).astype(BF16)
        fourier_ref[rows, orders:] = (-(sine * fine_cos + cosine * fine_sin)).astype(BF16)


def write_spectra(send_ref, slot, real, imaginary):
    members, _, owned, _ = send_ref.shape
    flipped = jnp.concatenate([real, imaginary], axis=0).T
    for device in range(members):
        send_ref[device, slot] = flipped[device * owned : (device + 1) * owned, :].astype(BF16)


def taps_of(weight_ref, dx):
    return jnp.concatenate([weight_ref[dy, dx] for dy in range(weight_ref.shape[0])], axis=0)


def shifted_sum(partial_ref, rows, height, first, count):
    taps = rows // height
    radius = taps // 2
    total = None
    for dx in range(taps):
        start = dx * height + first
        piece = partial_ref[start : start + count, :]
        if dx != radius:
            piece = pltpu.roll(piece, (radius - dx) % piece.shape[1], 1)
        total = piece if total is None else total + piece
    return total


def picked(group, radius, groups, field_ref, crossing):
    block = field_ref.shape[0] // groups
    height = block // group
    depth = radius * group
    shape = (depth, block)
    place, column = iota(shape, 0), iota(shape, 1)
    far = (lax.axis_index("lat") + crossing) % 2 == 0
    row = place % radius + jnp.where(far, height - radius, 0)
    chosen = column == place // radius * height + row
    selector = chosen.astype(F32).astype(BF16)
    for g in range(groups):
        yield dot_nn(selector, field_ref[g * block : (g + 1) * block, :]).astype(BF16)


def cross_kernel(group, radius, groups, field_ref, kept_ref, *cross_refs):
    depth = radius * group
    slots = [(ref, at) for ref in cross_refs for at in range(ref.shape[0] // depth)]
    for (ref, at), rows in zip(slots, picked(group, radius, groups, field_ref, 1)):
        ref[at * depth : (at + 1) * depth, :] = rows
    kept_ref[...] = field_ref[...]


def pair_kernel(group, radius, groups, field_ref, pair_ref):
    depth = radius * group
    for g, rows in enumerate(picked(group, radius, groups, field_ref, 0)):
        pair_ref[g * depth : (g + 1) * depth, :] = rows


def interior_kernel(
    group, weight_ref, bias_ref, field_ref,
    edge_ref, rim_ref, fourier_ref, send_ref,
    band_ref, partial_ref, hidden_ref, spectra_ref, column_ref,
):
    taps = weight_ref.shape[0]
    radius = taps // 2
    channels = weight_ref.shape[3]
    groups = channels // group
    height = field_ref.shape[0] // channels
    orders = fourier_ref.shape[1] // 2
    inner = height - 2 * radius
    block = height * group
    rows = taps * block

    write_fourier(fourier_ref, field_ref.shape[1], orders)
    shape = (channels, channels)
    bias = jnp.where(iota(shape, 0) == iota(shape, 1), bias_ref[...], 0.0)
    column_ref[...] = jnp.broadcast_to(jnp.sum(bias, axis=1, keepdims=True), column_ref.shape)
    shape = (taps * group, height * block)
    place = iota(shape, 0)
    column = iota(shape, 1)
    out_row, column = column // block, column % block
    chosen = (place % group == column // height) & (place // group == column % height - out_row + radius)
    selector = chosen.astype(F32).astype(BF16)
    position = lax.axis_index("lat")
    parity = position % 2
    polar = (position == 0) | (position == lax.axis_size("lat") - 1)
    open_side = jnp.where(polar, 0.0, 1.0)
    depth = radius * group
    rim_shape = (taps * group, 2 * depth)
    rim_place = iota(rim_shape, 0)
    rim_column = iota(rim_shape, 1)
    same = rim_place % group == rim_column % depth // radius
    rim_row = rim_column % radius
    rim_rows = taps * radius * group
    for dx in range(taps):
        mine = taps_of(weight_ref, dx)
        spread = dot_tn(mine, selector).astype(BF16)
        for g in range(groups):
            for row in range(height):
                start = g * rows + dx * block + row * group
                band_ref[start : start + group, :] = spread[
                    g * group : (g + 1) * group, row * block : (row + 1) * block
                ]
        for which in range(2):
            side = 1 - parity if which == 0 else parity
            for row in range(radius):
                tap = rim_row - row + side * (taps - 1)
                own = same & (rim_column // depth == which) & (rim_place // group == tap)
                pick = jnp.where(own, 1.0 if which == 0 else open_side, 0.0)
                spread = dot_tn(mine, pick.astype(BF16)).astype(BF16)
                for g in range(groups):
                    start = (g * 2 + which) * rim_rows + (dx * radius + row) * group
                    rim_ref[start : start + group, :] = spread[g * group : (g + 1) * group, :]

    def per_group(g, carry):
        band = band_ref[pl.ds(pl.multiple_of(g * rows, 16), rows), :]
        field = field_ref[pl.ds(pl.multiple_of(g * block, 16), block), :]
        partial_ref[...] = dot_nn(band, field)
        mine = pl.ds(pl.multiple_of(g * group, 16), group)
        bias = column_ref[mine, :][:, :1]
        for row in range(height):
            total = shifted_sum(partial_ref, rows, block, row * group, group) + bias
            if radius <= row < height - radius:
                start = pl.multiple_of((row - radius) * channels + g * group, 16)
                hidden_ref[pl.ds(start, group), :] = gelu(total).astype(BF16)
            else:
                edge_ref[row if row < radius else row - inner, mine, :] = total
        return carry

    lax.fori_loop(0, groups, per_group, 0)

    found = dot_nn(field_ref[...], fourier_ref[...])
    pitch = height + 1
    total = pitch * channels
    for part in range(2):
        for channel in range(channels):
            start = part * total + channel * pitch
            spectra_ref[start : start + height, :] = found[
                channel * height : (channel + 1) * height, part * orders : (part + 1) * orders
            ]
    for row in range(height):
        real, imaginary = (
            spectra_ref[pl.ds(part * total + row, channels, stride=pitch), :] for part in range(2)
        )
        write_spectra(send_ref, row, real, imaginary)
    found = dot_nn(hidden_ref[...], fourier_ref[...])
    for row in range(inner):
        mine = found[row * channels : (row + 1) * channels, :]
        write_spectra(send_ref, height + row, mine[:, :orders], mine[:, orders:])


def write_rim(group, radius, groups, rim_ref, edge_ref, pair_ref, cross_ref, partial_ref, store):
    rows = partial_ref.shape[0]
    depth = radius * group
    parity = lax.axis_index("lat") % 2

    def per_group(at, carry):
        g = groups[0] + at
        rim = rim_ref[pl.ds(pl.multiple_of(g * rows, 16), rows), :]
        pair = pair_ref[pl.ds(pl.multiple_of(g * depth, 16), depth), :]
        cross = cross_ref[pl.ds(pl.multiple_of(at * depth, 16), depth), :]
        partial_ref[...] = dot_nn(rim, jnp.concatenate([pair, cross], axis=0))
        for which, side in ((0, 1 - parity), (1, parity)):
            mine_ref = partial_ref.at[which * rows // 2 : (which + 1) * rows // 2]
            for row in range(radius):
                total = shifted_sum(mine_ref, rows // 2, depth, row * group, group)
                place = side * radius + row
                total = total + edge_ref[place, pl.ds(pl.multiple_of(g * group, 16), group), :]
                store(place, g, at, gelu(total).astype(BF16))
        return carry

    lax.fori_loop(0, groups[1] - groups[0], per_group, 0)


def first_rim_kernel(group, radius, groups, rim_ref, edge_ref, pair_ref, cross_ref, hidden_ref, partial_ref):
    def store(place, g, at, value):
        hidden_ref[place, pl.ds(pl.multiple_of(at * group, 16), group), :] = value

    write_rim(group, radius, groups, rim_ref, edge_ref, pair_ref, cross_ref, partial_ref, store)


def last_rim_kernel(
    group, radius, groups, rim_ref, edge_ref, pair_ref, cross_ref, fourier_ref, early_ref, *refs
):
    before_refs, (send_hbm, partial_ref, hidden_ref, late_ref, semaphores) = refs[:-5], refs[-5:]
    channels = edge_ref.shape[1]
    orders = fourier_ref.shape[1] // 2
    early = early_ref.shape[1]
    first = pltpu.make_async_copy(early_ref, send_hbm.at[:, pl.ds(0, early)], semaphores.at[0])
    first.start()
    for place in range(2 * radius):
        for before_ref in before_refs:
            size = before_ref.shape[1]
            hidden_ref[place * channels : place * channels + size, :] = before_ref[place]

    def store(place, g, at, value):
        start = pl.multiple_of(place * channels + g * group, 16)
        hidden_ref[pl.ds(start, group), :] = value

    write_rim(group, radius, groups, rim_ref, edge_ref, pair_ref, cross_ref, partial_ref, store)
    found = dot_nn(hidden_ref[...], fourier_ref[...])
    for row in range(2 * radius):
        mine = found[row * channels : (row + 1) * channels, :]
        write_spectra(late_ref, row, mine[:, :orders], mine[:, orders:])
    last = pltpu.make_async_copy(late_ref, send_hbm.at[:, pl.ds(early, 2 * radius)], semaphores.at[1])
    last.start()
    first.wait()
    last.wait()


def tables_kernel(
    group, turn_ref, sphere_ref, weight_ref,
    table_ref,
    steps_ref, rate_ref, base_ref, turned_ref,
):
    taps = weight_ref.shape[0]
    radius = taps // 2
    channels = weight_ref.shape[3]
    degrees = rate_ref.shape[0] // 2
    owned = table_ref.shape[0]
    wide = 2 * channels
    head = sphere_ref.shape[1]
    places = head * LANES // owned
    first_order = lax.axis_index("lat") * owned + 1

    shape = (degrees, LANES)
    order = (iota(shape, 1) % owned + first_order).astype(F32)
    degree = iota(shape, 0).astype(F32)
    previous = degree - 1.0
    raising = jnp.sqrt(
        jnp.maximum(4.0 * degree * degree - 1.0, 1.0) / jnp.maximum(degree * degree - order * order, 1.0)
    )
    lowering = jnp.sqrt(
        jnp.maximum(previous * previous - order * order, 0.0)
        / jnp.maximum(4.0 * previous * previous - 1.0, 1.0)
    )
    rate_ref[:degrees, :] = raising
    rate_ref[degrees:, :] = lowering

    shape = (ORDERS, LANES)
    number = (iota(shape, 0) + 1).astype(F32)
    ratio = jnp.where(
        iota(shape, 0) < iota(shape, 1) % owned + first_order, jnp.log((2.0 * number - 1.0) / (2.0 * number)), 0.0
    )
    log_ratio = jnp.sum(ratio, axis=0, keepdims=True)
    shape = (head, LANES)
    whole_order = iota(shape, 1) % owned + first_order
    order = whole_order.astype(F32)
    cosine, log_sine, quadrature = sphere_ref[0], sphere_ref[1], sphere_ref[2]
    diagonal = jnp.exp(0.5 * (jnp.log((2.0 * order + 1.0) / 2.0) + log_ratio) + order * log_sine)

    twice = (iota((channels, wide), 1) // 2 == iota((channels, wide), 0)).astype(F32).astype(BF16)
    across = (iota((group, wide), 1) % group == iota((group, wide), 0)).astype(F32).astype(BF16)
    shape = (wide, wide)
    row, column = iota(shape, 0), iota(shape, 1)
    row_part, column_part = row // channels, column % 2
    same_group = row % channels // group == column // 2 // group
    straight = row_part == column_part
    sign = jnp.where(column_part > row_part, 1.0, -1.0)
    flat = jnp.concatenate([weight_ref[dy, dx] for dy in range(taps) for dx in range(taps)], axis=0)
    doubled = dot_nn(flat, twice).astype(BF16)

    def expanded(dy, dx):
        start = (dy * taps + dx) * group
        return dot_tn(across, doubled[start : start + group, :])

    for dy in range(taps):
        tap = [expanded(dy, dx) for dx in range(taps)]
        base_ref[dy, 0] = jnp.where(same_group & straight, tap[radius], 0.0)
        for far in range(1, radius + 1):
            high, low = tap[radius + far], tap[radius - far]
            both = jnp.where(straight, high + low, sign * (high - low))
            base_ref[dy, far] = jnp.where(same_group, both, 0.0)
    steps = degrees // owned

    def per_order(k, carried):
        latest, before = carried
        for step in range(steps):
            at = k * steps + step
            up = jnp.broadcast_to(rate_ref[pl.ds(at, 1), :], (head, LANES))
            down = jnp.broadcast_to(rate_ref[pl.ds(degrees + at, 1), :], (head, LANES))
            raised = up * (cosine * latest - down * before)
            latest, before = jnp.where(whole_order == at, diagonal, raised), latest
            steps_ref[pl.ds(pl.multiple_of(at * head, 8), head), :] = latest * quadrature
        factors = [
            jnp.where(straight, turn_ref[2 * far, k], turn_ref[2 * far + 1, k]) for far in range(radius)
        ]
        for dy in range(taps):
            total = base_ref[dy, 0]
            for far in range(radius):
                total = total + base_ref[dy, far + 1] * factors[far]
            table_ref[k, dy * wide : (dy + 1) * wide, :wide] = total.astype(BF16)
        return latest, before

    nothing = order * cosine * 0.0
    lax.fori_loop(0, owned, per_order, (nothing, nothing))
    half = degrees // 2
    total = head * LANES
    for parity in range(2):
        for at in range(head):
            mine = steps_ref[pl.ds(parity * head + at, half, stride=2 * head), :]
            turned_ref[parity * total + at * LANES : parity * total + (at + 1) * LANES, :] = mine.T
    for parity in range(2):
        for k in range(owned):
            mine = turned_ref[pl.ds(parity * total + k, places, stride=owned), :]
            start = taps * wide + parity * places
            table_ref[k, start : start + places, :half] = mine.astype(BF16)


def project_kernel(
    radius, got_ref, table_ref, out_hbm, rows_ref, plain_ref, out_ref, semaphores
):
    members, height, owned, wide = got_ref.shape
    height = height // 2
    places = members * height
    pitch = owned + 1
    pad = radius * pitch
    taps = 2 * radius + 1

    rows_ref[:pad, :] = jnp.zeros((pad, rows_ref.shape[1]), F32)
    rows_ref[pad + places * pitch :, :] = jnp.zeros((pad, rows_ref.shape[1]), F32)
    for source in range(members):
        for row in range(height):
            start = (source * height + row) * pitch
            plain_ref[start : start + owned, :wide] = got_ref[source, row].astype(F32)
            if radius <= row < height - radius:
                place = height + row - radius
            elif row < radius:
                place = 2 * height - 2 * radius + row
            else:
                place = height + row
            rows_ref[pad + start : pad + start + owned, :wide] = got_ref[source, place].astype(F32)

    row, column = iota((wide, wide), 0), iota((wide, wide), 1)
    identity = (row == column % 2 * (wide // 2) + column // 2).astype(F32).astype(BF16)
    identity = jnp.concatenate([identity] * (2 if owned % 2 == 0 else 1), axis=1)
    mix = taps * wide
    half = out_ref.shape[3]

    def sent(k):
        return pltpu.make_async_copy(out_ref.at[k], out_hbm.at[k], semaphores.at[k])

    def gathered(k):
        pieces = [rows_ref[pl.ds(dy * pitch + k, places, stride=pitch), :] for dy in range(taps)]
        pieces.append(plain_ref[pl.ds(k, places, stride=pitch), :])
        return jnp.concatenate([piece[:, :wide].astype(BF16) for piece in pieces], axis=1)

    together = 2 if owned % 2 == 0 else 1
    for first in range(0, owned, together):
        orders = range(first, first + together)
        stacked = jnp.concatenate([gathered(k) for k in orders], axis=0)
        mixing = jnp.concatenate([table_ref[k, :mix, :wide] for k in orders], axis=1)
        mixing = jnp.concatenate([mixing, identity], axis=0)
        both = dot_nn(stacked, mixing)
        for at, k in enumerate(orders):
            mixed = both[at * places : (at + 1) * places, at * wide : (at + 1) * wide].T.astype(BF16)
            legendre = jnp.concatenate(
                [table_ref[k, mix + q * places : mix + (q + 1) * places, :half] for q in range(2)], axis=1
            )
            found = dot_nn(mixed, legendre)
            out_ref[k, 0] = found[:, :half]
            out_ref[k, 1] = found[:, half:]
            sent(k).start()
    for k in range(owned):
        sent(k).wait()


def per_device(atmosphere, first_weight, first_bias, second_weight):
    members = lax.axis_size("lat")
    position = lax.axis_index("lat")
    channels, height, length = atmosphere.shape
    group, taps = first_weight.shape[1], first_weight.shape[3]
    radius = taps // 2
    groups = channels // group
    inner = height - 2 * radius
    owned = ORDERS // members
    wide = 2 * channels
    places = height * members

    shapes = jax.ShapeDtypeStruct
    block = height * group
    rim_rows = taps * radius * group
    first_taps = first_weight.transpose(2, 3, 1, 0)
    second_taps = second_weight.transpose(2, 3, 1, 0)
    flat = atmosphere.reshape(channels * height, length)
    share = -(-groups // 4)
    parts = [count for count in (groups - share, share) if count]
    flat, *crossed = call(
        lambda *refs: cross_kernel(group, radius, groups, *refs),
        "cross_rows",
        (shapes(flat.shape, BF16),) + tuple(shapes((p * group * radius, length), BF16) for p in parts),
        [],
        6,
        2 * radius * channels * block * length,
        (flat,),
    )
    crosses = [(i, (i + 1 if i % 2 else i - 1) % members) for i in range(members)]
    crossed = [lax.ppermute(cross, "lat", crosses) for cross in crossed]
    pair = call(
        lambda *refs: pair_kernel(group, radius, groups, *refs),
        "pair_rows",
        shapes((channels * radius, length), BF16),
        [],
        6,
        2 * radius * channels * block * length,
        (flat,),
    )
    pairs = [(i, i ^ 1) for i in range(members) if i ^ 1 < members]
    pair = lax.ppermute(pair, "lat", pairs)

    edge, rim, fourier, early = call(
        lambda *refs: interior_kernel(group, *refs),
        "interior",
        (
            shapes((2 * radius, channels, length), F32),
            shapes((groups * 2 * rim_rows, 2 * radius * group), BF16),
            shapes((length, 2 * ORDERS), BF16),
            shapes((members, height + inner, owned, wide), BF16),
        ),
        [
            pltpu.VMEM((groups * taps * block, block), BF16),
            pltpu.VMEM((taps * block, length), F32),
            pltpu.VMEM((inner * channels, length), BF16),
            pltpu.VMEM((2 * (height + 1) * channels, ORDERS), F32),
            pltpu.VMEM((channels, LANES), F32),
        ],
        10,
        2 * taps * block * block * length * groups,
        (first_taps, first_bias[None, :], flat),
    )
    partial = pltpu.VMEM((2 * rim_rows, length), F32)
    flops = 8 * rim_rows * radius * group * length * share
    before = [
        call(
            lambda *refs: first_rim_kernel(group, radius, (0, groups - share), *refs),
            "rim_first",
            shapes((2 * radius, (groups - share) * group, length), BF16),
            [partial],
            6,
            flops,
            (rim, edge, pair, cross),
        )
        for cross in crossed[:-1]
    ]
    send = call(
        lambda *refs: last_rim_kernel(group, radius, (groups - share, groups), *refs),
        "rim_last",
        shapes((members, 2 * height, owned, wide), BF16),
        [
            partial,
            pltpu.VMEM((2 * radius * channels, length), BF16),
            pltpu.VMEM((members, 2 * radius, owned, wide), BF16),
            pltpu.SemaphoreType.DMA((2,)),
        ],
        8,
        flops,
        (rim, edge, pair, crossed[-1], fourier, early, *before),
        out_specs=HBM,
    )
    got = lax.all_to_all(send, "lat", 0, 0, tiled=True)

    angle = (position * owned + 1 + jnp.arange(owned, dtype=jnp.int32)).astype(F32) * (2.0 * math.pi / length)
    turns = jnp.stack([f(far * angle) for far in range(1, radius + 1) for f in (jnp.cos, jnp.sin)])
    colatitude = np.pi * (np.arange(places) + 0.5) / places
    cosine = np.cos(colatitude)
    cosine[places // 2 :] = -cosine[: places // 2][::-1]
    sine = np.sin(np.minimum(colatitude, colatitude[::-1]))
    sphere = np.stack([cosine, np.log(sine), np.pi * sine / np.sqrt(places)]).astype(np.float32)
    head = places * owned // LANES
    sphere = np.repeat(sphere.reshape(3, head, LANES // owned), owned, axis=2)
    table = call(
        lambda *refs: tables_kernel(group, *refs),
        "tables",
        shapes((owned, taps * wide + 2 * places, max(wide, DEGREES // 2)), BF16),
        [
            pltpu.VMEM((DEGREES * head, LANES), F32),
            pltpu.VMEM((2 * DEGREES, LANES), F32),
            pltpu.VMEM((taps, radius + 1, wide, wide), F32),
            pltpu.VMEM((2 * head * LANES, DEGREES // 2), F32),
        ],
        6,
        2 * owned * wide * taps * wide * 8,
        (turns, jnp.asarray(sphere), second_taps),
        in_specs=[SMEM, VMEM, VMEM],
    )

    lanes = max(wide, LANES)
    spectrum = call(
        lambda *refs: project_kernel(radius, *refs),
        "project",
        shapes((owned, 2, wide, DEGREES // 2), F32),
        [
            pltpu.VMEM(((places + 2 * radius) * (owned + 1), lanes), F32),
            pltpu.VMEM((places * (owned + 1), lanes), F32),
            pltpu.VMEM((owned, 2, wide, DEGREES // 2), F32),
            pltpu.SemaphoreType.DMA((owned,)),
        ],
        6,
        2 * owned * wide * places * ((taps + 1) * wide + DEGREES),
        (got, table),
        out_specs=HBM,
    )
    return spectrum.reshape(owned, 2, channels, 2, DEGREES // 2)


def solution(mesh):
    placed = (
        P("chan", "lat", None),
        P("chan", None, None, None),
        P("chan"),
        P("chan", None, None, None),
    )
    return jax.shard_map(
        per_device,
        mesh=mesh,
        in_specs=placed,
        out_specs=P("lat", None, "chan", None, None),
        check_vma=False,
    )
```

```python
import math

import jax
import jax.numpy as jnp
import numpy as np
from jax import lax
from jax.experimental import pallas as pl
from jax.experimental.pallas import tpu as pltpu
from jax.sharding import PartitionSpec as P

ORDERS = 128
DEGREES = 256
LANES = 128
F32 = jnp.float32
BF16 = jnp.bfloat16


def dot_tn(left, right):
    return lax.dot_general(left, right, (((0,), (0,)), ((), ())), preferred_element_type=F32)


def dot_nn(left, right):
    return jnp.dot(left, right, preferred_element_type=F32)


def iota(shape, dim):
    return lax.broadcasted_iota(jnp.int32, shape, dim)


def gelu(value):
    return 0.5 * value * (1.0 + lax.erf(value * math.sqrt(0.5)))


VMEM = pl.BlockSpec(memory_space=pltpu.VMEM)
SMEM = pl.BlockSpec(memory_space=pltpu.SMEM)
HBM = pl.BlockSpec(memory_space=pltpu.HBM)


def bytes_of(arrays):
    return sum(math.prod(a.shape) * a.dtype.itemsize for a in jax.tree.leaves(arrays))


def call(kernel, out_shape, scratch, mebibytes, flops, args, in_specs=None, out_specs=None):
    size = bytes_of((args, out_shape))
    return pl.pallas_call(
        kernel,
        out_shape=out_shape,
        in_specs=in_specs or [VMEM] * len(args),
        out_specs=out_specs or jax.tree.map(lambda _: VMEM, out_shape),
        scratch_shapes=scratch,
        compiler_params=pltpu.CompilerParams(vmem_limit_bytes=mebibytes * 2**20),
        cost_estimate=pl.CostEstimate(flops=flops, transcendentals=0, bytes_accessed=size),
    )(*args)


def turned(number, length):
    number = number.astype(F32)
    number = number - length * jnp.floor(number / length)
    return number * (2.0 * math.pi / length)


def write_fourier(fourier_ref, length, orders):
    tile = 128
    factor = 1.0 / math.sqrt(length)
    shape = (tile, orders)
    fine = turned(iota(shape, 0) * (iota(shape, 1) + 1), length)
    fine_cos, fine_sin = jnp.cos(fine), jnp.sin(fine)
    blocks = length // tile
    padded = -(-blocks // 8) * 8
    shape = (padded, orders)
    coarse = turned(iota(shape, 0) * tile * (iota(shape, 1) + 1), length)
    coarse_cos, coarse_sin = jnp.cos(coarse) * factor, jnp.sin(coarse) * factor
    for block in range(blocks):
        cosine = coarse_cos[block : block + 1, :]
        sine = coarse_sin[block : block + 1, :]
        rows = slice(block * tile, (block + 1) * tile)
        fourier_ref[rows, :orders] = (cosine * fine_cos - sine * fine_sin).astype(BF16)
        fourier_ref[rows, orders:] = (-(sine * fine_cos + cosine * fine_sin)).astype(BF16)


def write_spectra(send_ref, slot, real, imaginary):
    members, _, owned, _ = send_ref.shape
    flipped = jnp.concatenate([real, imaginary], axis=0).T
    for device in range(members):
        send_ref[device, slot] = flipped[device * owned : (device + 1) * owned, :].astype(BF16)


def taps_of(weight_ref, dx):
    return jnp.concatenate([weight_ref[dy, dx] for dy in range(weight_ref.shape[0])], axis=0)


def shifted_sum(partial_ref, rows, height, first, count):
    taps = rows // height
    radius = taps // 2
    total = None
    for dx in range(taps):
        start = dx * height + first
        piece = partial_ref[start : start + count, :]
        if dx != radius:
            piece = pltpu.roll(piece, (radius - dx) % piece.shape[1], 1)
        total = piece if total is None else total + piece
    return total


def picked(group, radius, groups, field_ref, crossing):
    block = field_ref.shape[0] // groups
    height = block // group
    depth = radius * group
    shape = (depth, block)
    place, column = iota(shape, 0), iota(shape, 1)
    far = (lax.axis_index("lat") + crossing) % 2 == 0
    row = place % radius + jnp.where(far, height - radius, 0)
    chosen = column == place // radius * height + row
    selector = chosen.astype(F32).astype(BF16)
    for g in range(groups):
        yield dot_nn(selector, field_ref[g * block : (g + 1) * block, :]).astype(BF16)


def cross_kernel(group, radius, groups, field_ref, kept_ref, *cross_refs):
    depth = radius * group
    slots = [(ref, at) for ref in cross_refs for at in range(ref.shape[0] // depth)]
    for (ref, at), rows in zip(slots, picked(group, radius, groups, field_ref, 1)):
        ref[at * depth : (at + 1) * depth, :] = rows
    kept_ref[...] = field_ref[...]


def pair_kernel(group, radius, groups, field_ref, pair_ref):
    depth = radius * group
    for g, rows in enumerate(picked(group, radius, groups, field_ref, 0)):
        pair_ref[g * depth : (g + 1) * depth, :] = rows


def interior_kernel(
    group, weight_ref, bias_ref, field_ref,
    edge_ref, rim_ref, fourier_ref, send_ref,
    band_ref, partial_ref, hidden_ref, spectra_ref, column_ref,
):
    taps = weight_ref.shape[0]
    radius = taps // 2
    channels = weight_ref.shape[3]
    groups = channels // group
    height = field_ref.shape[0] // channels
    orders = fourier_ref.shape[1] // 2
    inner = height - 2 * radius
    block = height * group
    rows = taps * block

    write_fourier(fourier_ref, field_ref.shape[1], orders)
    shape = (channels, channels)
    bias = jnp.where(iota(shape, 0) == iota(shape, 1), bias_ref[...], 0.0)
    column_ref[...] = jnp.broadcast_to(jnp.sum(bias, axis=1, keepdims=True), column_ref.shape)
    shape = (taps * group, height * block)
    place = iota(shape, 0)
    column = iota(shape, 1)
    out_row, column = column // block, column % block
    chosen = (place % group == column // height) & (place // group == column % height - out_row + radius)
    selector = chosen.astype(F32).astype(BF16)
    position = lax.axis_index("lat")
    parity = position % 2
    polar = (position == 0) | (position == lax.axis_size("lat") - 1)
    open_side = jnp.where(polar, 0.0, 1.0)
    depth = radius * group
    rim_shape = (taps * group, 2 * depth)
    rim_place = iota(rim_shape, 0)
    rim_column = iota(rim_shape, 1)
    same = rim_place % group == rim_column % depth // radius
    rim_row = rim_column % radius
    rim_rows = taps * radius * group
    for dx in range(taps):
        mine = taps_of(weight_ref, dx)
        spread = dot_tn(mine, selector).astype(BF16)
        for g in range(groups):
            for row in range(height):
                start = g * rows + dx * block + row * group
                band_ref[start : start + group, :] = spread[
                    g * group : (g + 1) * group, row * block : (row + 1) * block
                ]
        for which in range(2):
            side = 1 - parity if which == 0 else parity
            for row in range(radius):
                tap = rim_row - row + side * (taps - 1)
                own = same & (rim_column // depth == which) & (rim_place // group == tap)
                pick = jnp.where(own, 1.0 if which == 0 else open_side, 0.0)
                spread = dot_tn(mine, pick.astype(BF16)).astype(BF16)
                for g in range(groups):
                    start = (g * 2 + which) * rim_rows + (dx * radius + row) * group
                    rim_ref[start : start + group, :] = spread[g * group : (g + 1) * group, :]

    def per_group(g, carry):
        band = band_ref[pl.ds(pl.multiple_of(g * rows, 16), rows), :]
        field = field_ref[pl.ds(pl.multiple_of(g * block, 16), block), :]
        partial_ref[...] = dot_nn(band, field)
        mine = pl.ds(pl.multiple_of(g * group, 16), group)
        bias = column_ref[mine, :][:, :1]
        for row in range(height):
            total = shifted_sum(partial_ref, rows, block, row * group, group) + bias
            if radius <= row < height - radius:
                start = pl.multiple_of((row - radius) * channels + g * group, 16)
                hidden_ref[pl.ds(start, group), :] = gelu(total).astype(BF16)
            else:
                edge_ref[row if row < radius else row - inner, mine, :] = total
        return carry

    lax.fori_loop(0, groups, per_group, 0)

    found = dot_nn(field_ref[...], fourier_ref[...])
    pitch = height + 1
    total = pitch * channels
    for part in range(2):
        for channel in range(channels):
            start = part * total + channel * pitch
            spectra_ref[start : start + height, :] = found[
                channel * height : (channel + 1) * height, part * orders : (part + 1) * orders
            ]
    for row in range(height):
        real, imaginary = (
            spectra_ref[pl.ds(part * total + row, channels, stride=pitch), :] for part in range(2)
        )
        write_spectra(send_ref, row, real, imaginary)
    found = dot_nn(hidden_ref[...], fourier_ref[...])
    for row in range(inner):
        mine = found[row * channels : (row + 1) * channels, :]
        write_spectra(send_ref, height + row, mine[:, :orders], mine[:, orders:])


def write_rim(group, radius, groups, rim_ref, edge_ref, pair_ref, cross_ref, partial_ref, store):
    rows = partial_ref.shape[0]
    depth = radius * group
    parity = lax.axis_index("lat") % 2

    def per_group(at, carry):
        g = groups[0] + at
        rim = rim_ref[pl.ds(pl.multiple_of(g * rows, 16), rows), :]
        pair = pair_ref[pl.ds(pl.multiple_of(g * depth, 16), depth), :]
        cross = cross_ref[pl.ds(pl.multiple_of(at * depth, 16), depth), :]
        partial_ref[...] = dot_nn(rim, jnp.concatenate([pair, cross], axis=0))
        for which, side in ((0, 1 - parity), (1, parity)):
            mine_ref = partial_ref.at[which * rows // 2 : (which + 1) * rows // 2]
            for row in range(radius):
                total = shifted_sum(mine_ref, rows // 2, depth, row * group, group)
                place = side * radius + row
                total = total + edge_ref[place, pl.ds(pl.multiple_of(g * group, 16), group), :]
                store(place, g, at, gelu(total).astype(BF16))
        return carry

    lax.fori_loop(0, groups[1] - groups[0], per_group, 0)


def first_rim_kernel(group, radius, groups, rim_ref, edge_ref, pair_ref, cross_ref, hidden_ref, partial_ref):
    def store(place, g, at, value):
        hidden_ref[place, pl.ds(pl.multiple_of(at * group, 16), group), :] = value

    write_rim(group, radius, groups, rim_ref, edge_ref, pair_ref, cross_ref, partial_ref, store)


def last_rim_kernel(
    group, radius, groups, rim_ref, edge_ref, pair_ref, cross_ref, fourier_ref, early_ref, *refs
):
    before_refs, (send_hbm, partial_ref, hidden_ref, late_ref, semaphores) = refs[:-5], refs[-5:]
    channels = edge_ref.shape[1]
    orders = fourier_ref.shape[1] // 2
    early = early_ref.shape[1]
    first = pltpu.make_async_copy(early_ref, send_hbm.at[:, pl.ds(0, early)], semaphores.at[0])
    first.start()
    for place in range(2 * radius):
        for before_ref in before_refs:
            size = before_ref.shape[1]
            hidden_ref[place * channels : place * channels + size, :] = before_ref[place]

    def store(place, g, at, value):
        start = pl.multiple_of(place * channels + g * group, 16)
        hidden_ref[pl.ds(start, group), :] = value

    write_rim(group, radius, groups, rim_ref, edge_ref, pair_ref, cross_ref, partial_ref, store)
    found = dot_nn(hidden_ref[...], fourier_ref[...])
    for row in range(2 * radius):
        mine = found[row * channels : (row + 1) * channels, :]
        write_spectra(late_ref, row, mine[:, :orders], mine[:, orders:])
    last = pltpu.make_async_copy(late_ref, send_hbm.at[:, pl.ds(early, 2 * radius)], semaphores.at[1])
    last.start()
    first.wait()
    last.wait()


def tables_kernel(
    group, turn_ref, sphere_ref, weight_ref,
    table_ref,
    steps_ref, rate_ref, base_ref, turned_ref,
):
    taps = weight_ref.shape[0]
    radius = taps // 2
    channels = weight_ref.shape[3]
    degrees = rate_ref.shape[0] // 2
    owned = table_ref.shape[0]
    wide = 2 * channels
    head = sphere_ref.shape[1]
    places = head * LANES // owned
    first_order = lax.axis_index("lat") * owned + 1

    shape = (degrees, LANES)
    order = (iota(shape, 1) % owned + first_order).astype(F32)
    degree = iota(shape, 0).astype(F32)
    previous = degree - 1.0
    raising = jnp.sqrt(
        jnp.maximum(4.0 * degree * degree - 1.0, 1.0) / jnp.maximum(degree * degree - order * order, 1.0)
    )
    lowering = jnp.sqrt(
        jnp.maximum(previous * previous - order * order, 0.0)
        / jnp.maximum(4.0 * previous * previous - 1.0, 1.0)
    )
    rate_ref[:degrees, :] = raising
    rate_ref[degrees:, :] = lowering

    shape = (ORDERS, LANES)
    number = (iota(shape, 0) + 1).astype(F32)
    ratio = jnp.where(
        iota(shape, 0) < iota(shape, 1) % owned + first_order, jnp.log((2.0 * number - 1.0) / (2.0 * number)), 0.0
    )
    log_ratio = jnp.sum(ratio, axis=0, keepdims=True)
    shape = (head, LANES)
    whole_order = iota(shape, 1) % owned + first_order
    order = whole_order.astype(F32)
    cosine, log_sine, quadrature = sphere_ref[0], sphere_ref[1], sphere_ref[2]
    diagonal = jnp.exp(0.5 * (jnp.log((2.0 * order + 1.0) / 2.0) + log_ratio) + order * log_sine)

    twice = (iota((channels, wide), 1) // 2 == iota((channels, wide), 0)).astype(F32).astype(BF16)
    across = (iota((group, wide), 1) % group == iota((group, wide), 0)).astype(F32).astype(BF16)
    shape = (wide, wide)
    row, column = iota(shape, 0), iota(shape, 1)
    row_part, column_part = row // channels, column % 2
    same_group = row % channels // group == column // 2 // group
    straight = row_part == column_part
    sign = jnp.where(column_part > row_part, 1.0, -1.0)
    flat = jnp.concatenate([weight_ref[dy, dx] for dy in range(taps) for dx in range(taps)], axis=0)
    doubled = dot_nn(flat, twice).astype(BF16)

    def expanded(dy, dx):
        start = (dy * taps + dx) * group
        return dot_tn(across, doubled[start : start + group, :])

    for dy in range(taps):
        tap = [expanded(dy, dx) for dx in range(taps)]
        base_ref[dy, 0] = jnp.where(same_group & straight, tap[radius], 0.0)
        for far in range(1, radius + 1):
            high, low = tap[radius + far], tap[radius - far]
            both = jnp.where(straight, high + low, sign * (high - low))
            base_ref[dy, far] = jnp.where(same_group, both, 0.0)
    steps = degrees // owned

    def per_order(k, carried):
        latest, before = carried
        for step in range(steps):
            at = k * steps + step
            up = jnp.broadcast_to(rate_ref[pl.ds(at, 1), :], (head, LANES))
            down = jnp.broadcast_to(rate_ref[pl.ds(degrees + at, 1), :], (head, LANES))
            raised = up * (cosine * latest - down * before)
            latest, before = jnp.where(whole_order == at, diagonal, raised), latest
            steps_ref[pl.ds(pl.multiple_of(at * head, 8), head), :] = latest * quadrature
        factors = [
            jnp.where(straight, turn_ref[2 * far, k], turn_ref[2 * far + 1, k]) for far in range(radius)
        ]
        for dy in range(taps):
            total = base_ref[dy, 0]
            for far in range(radius):
                total = total + base_ref[dy, far + 1] * factors[far]
            table_ref[k, dy * wide : (dy + 1) * wide, :wide] = total.astype(BF16)
        return latest, before

    nothing = order * cosine * 0.0
    lax.fori_loop(0, owned, per_order, (nothing, nothing))
    half = degrees // 2
    total = head * LANES
    for parity in range(2):
        for at in range(head):
            mine = steps_ref[pl.ds(parity * head + at, half, stride=2 * head), :]
            turned_ref[parity * total + at * LANES : parity * total + (at + 1) * LANES, :] = mine.T
    for parity in range(2):
        for k in range(owned):
            mine = turned_ref[pl.ds(parity * total + k, places, stride=owned), :]
            start = taps * wide + parity * places
            table_ref[k, start : start + places, :half] = mine.astype(BF16)


def project_kernel(
    radius, got_ref, table_ref, out_hbm, rows_ref, plain_ref, out_ref, semaphores
):
    members, height, owned, wide = got_ref.shape
    height = height // 2
    places = members * height
    pitch = owned + 1
    pad = radius * pitch
    taps = 2 * radius + 1

    rows_ref[:pad, :] = jnp.zeros((pad, rows_ref.shape[1]), F32)
    rows_ref[pad + places * pitch :, :] = jnp.zeros((pad, rows_ref.shape[1]), F32)
    for source in range(members):
        for row in range(height):
            start = (source * height + row) * pitch
            plain_ref[start : start + owned, :wide] = got_ref[source, row].astype(F32)
            if radius <= row < height - radius:
                place = height + row - radius
            elif row < radius:
                place = 2 * height - 2 * radius + row
            else:
                place = height + row
            rows_ref[pad + start : pad + start + owned, :wide] = got_ref[source, place].astype(F32)

    row, column = iota((wide, wide), 0), iota((wide, wide), 1)
    identity = (row == column % 2 * (wide // 2) + column // 2).astype(F32).astype(BF16)
    identity = jnp.concatenate([identity] * (2 if owned % 2 == 0 else 1), axis=1)
    mix = taps * wide
    half = out_ref.shape[3]

    def sent(k):
        return pltpu.make_async_copy(out_ref.at[k], out_hbm.at[k], semaphores.at[k])

    def gathered(k):
        pieces = [rows_ref[pl.ds(dy * pitch + k, places, stride=pitch), :] for dy in range(taps)]
        pieces.append(plain_ref[pl.ds(k, places, stride=pitch), :])
        return jnp.concatenate([piece[:, :wide].astype(BF16) for piece in pieces], axis=1)

    together = 2 if owned % 2 == 0 else 1
    for first in range(0, owned, together):
        orders = range(first, first + together)
        stacked = jnp.concatenate([gathered(k) for k in orders], axis=0)
        mixing = jnp.concatenate([table_ref[k, :mix, :wide] for k in orders], axis=1)
        mixing = jnp.concatenate([mixing, identity], axis=0)
        both = dot_nn(stacked, mixing)
        for at, k in enumerate(orders):
            mixed = both[at * places : (at + 1) * places, at * wide : (at + 1) * wide].T.astype(BF16)
            legendre = jnp.concatenate(
                [table_ref[k, mix + q * places : mix + (q + 1) * places, :half] for q in range(2)], axis=1
            )
            found = dot_nn(mixed, legendre)
            out_ref[k, 0] = found[:, :half]
            out_ref[k, 1] = found[:, half:]
            sent(k).start()
    for k in range(owned):
        sent(k).wait()


def per_device(atmosphere, first_weight, first_bias, second_weight):
    members = lax.axis_size("lat")
    position = lax.axis_index("lat")
    channels, height, length = atmosphere.shape
    group, taps = first_weight.shape[1], first_weight.shape[3]
    radius = taps // 2
    groups = channels // group
    inner = height - 2 * radius
    owned = ORDERS // members
    wide = 2 * channels
    places = height * members

    shapes = jax.ShapeDtypeStruct
    block = height * group
    rim_rows = taps * radius * group
    first_taps = first_weight.transpose(2, 3, 1, 0)
    second_taps = second_weight.transpose(2, 3, 1, 0)
    flat = atmosphere.reshape(channels * height, length)
    share = -(-groups // 4)
    parts = [count for count in (groups - share, share) if count]
    flat, *crossed = call(
        lambda *refs: cross_kernel(group, radius, groups, *refs),
        (shapes(flat.shape, BF16),) + tuple(shapes((p * group * radius, length), BF16) for p in parts),
        [],
        6,
        2 * radius * channels * block * length,
        (flat,),
    )
    crosses = [(i, (i + 1 if i % 2 else i - 1) % members) for i in range(members)]
    for at, cross in enumerate(crossed):
        crossed[at] = lax.ppermute(cross, "lat", crosses)
    pair = call(
        lambda *refs: pair_kernel(group, radius, groups, *refs),
        shapes((channels * radius, length), BF16),
        [],
        6,
        2 * radius * channels * block * length,
        (flat,),
    )
    pairs = [(i, i ^ 1) for i in range(members) if i ^ 1 < members]
    pair = lax.ppermute(pair, "lat", pairs)

    edge, rim, fourier, early = call(
        lambda *refs: interior_kernel(group, *refs),
        (
            shapes((2 * radius, channels, length), F32),
            shapes((groups * 2 * rim_rows, 2 * radius * group), BF16),
            shapes((length, 2 * ORDERS), BF16),
            shapes((members, height + inner, owned, wide), BF16),
        ),
        [
            pltpu.VMEM((groups * taps * block, block), BF16),
            pltpu.VMEM((taps * block, length), F32),
            pltpu.VMEM((inner * channels, length), BF16),
            pltpu.VMEM((2 * (height + 1) * channels, ORDERS), F32),
            pltpu.VMEM((channels, LANES), F32),
        ],
        10,
        2 * taps * block * block * length * groups,
        (first_taps, first_bias[None, :], flat),
    )
    partial = pltpu.VMEM((2 * rim_rows, length), F32)
    flops = 8 * rim_rows * radius * group * length * share
    before = [
        call(
            lambda *refs: first_rim_kernel(group, radius, (0, groups - share), *refs),
            shapes((2 * radius, (groups - share) * group, length), BF16),
            [partial],
            6,
            flops,
            (rim, edge, pair, cross),
        )
        for cross in crossed[:-1]
    ]
    send = call(
        lambda *refs: last_rim_kernel(group, radius, (groups - share, groups), *refs),
        shapes((members, 2 * height, owned, wide), BF16),
        [
            partial,
            pltpu.VMEM((2 * radius * channels, length), BF16),
            pltpu.VMEM((members, 2 * radius, owned, wide), BF16),
            pltpu.SemaphoreType.DMA((2,)),
        ],
        8,
        flops,
        (rim, edge, pair, crossed[-1], fourier, early, *before),
        out_specs=HBM,
    )
    got = lax.all_to_all(send, "lat", 0, 0, tiled=True)

    angle = (position * owned + 1 + jnp.arange(owned, dtype=jnp.int32)).astype(F32) * (2.0 * math.pi / length)
    turns = jnp.stack([f(far * angle) for far in range(1, radius + 1) for f in (jnp.cos, jnp.sin)])
    colatitude = np.pi * (np.arange(places) + 0.5) / places
    cosine = np.cos(colatitude)
    cosine[places // 2 :] = -cosine[: places // 2][::-1]
    sine = np.sin(np.minimum(colatitude, colatitude[::-1]))
    sphere = np.stack([cosine, np.log(sine), np.pi * sine / np.sqrt(places)]).astype(np.float32)
    head = places * owned // LANES
    sphere = np.repeat(sphere.reshape(3, head, LANES // owned), owned, axis=2)
    table = call(
        lambda *refs: tables_kernel(group, *refs),
        shapes((owned, taps * wide + 2 * places, max(wide, DEGREES // 2)), BF16),
        [
            pltpu.VMEM((DEGREES * head, LANES), F32),
            pltpu.VMEM((2 * DEGREES, LANES), F32),
            pltpu.VMEM((taps, radius + 1, wide, wide), F32),
            pltpu.VMEM((2 * head * LANES, DEGREES // 2), F32),
        ],
        6,
        2 * owned * wide * taps * wide * 8,
        (turns, jnp.asarray(sphere), second_taps),
        in_specs=[SMEM, VMEM, VMEM],
    )

    lanes = max(wide, LANES)
    spectrum = call(
        lambda *refs: project_kernel(radius, *refs),
        shapes((owned, 2, wide, DEGREES // 2), F32),
        [
            pltpu.VMEM(((places + 2 * radius) * (owned + 1), lanes), F32),
            pltpu.VMEM((places * (owned + 1), lanes), F32),
            pltpu.VMEM((owned, 2, wide, DEGREES // 2), F32),
            pltpu.SemaphoreType.DMA((owned,)),
        ],
        6,
        2 * owned * wide * places * ((taps + 1) * wide + DEGREES),
        (got, table),
        out_specs=HBM,
    )
    return spectrum.reshape(owned, 2, channels, 2, DEGREES // 2)


def solution(mesh):
    placed = (
        P("chan", "lat", None),
        P("chan", None, None, None),
        P("chan"),
        P("chan", None, None, None),
    )

    return jax.shard_map(
        per_device,
        mesh=mesh,
        in_specs=placed,
        out_specs=P("lat", None, "chan", None, None),
        check_vma=False,
    )
```

```python
import math

import jax
import jax.numpy as jnp
import numpy as np
from jax import lax
from jax.experimental import pallas as pl
from jax.experimental.pallas import tpu as pltpu
from jax.sharding import PartitionSpec as P

ORDERS = 128
DEGREES = 256
LANES = 128
F32 = jnp.float32
BF16 = jnp.bfloat16


def dot_tn(left, right):
    return lax.dot_general(left, right, (((0,), (0,)), ((), ())), preferred_element_type=F32)


def dot_nn(left, right):
    return jnp.dot(left, right, preferred_element_type=F32)


def iota(shape, dim):
    return lax.broadcasted_iota(jnp.int32, shape, dim)


def gelu(value):
    return 0.5 * value * (1.0 + lax.erf(value * math.sqrt(0.5)))


VMEM = pl.BlockSpec(memory_space=pltpu.VMEM)
SMEM = pl.BlockSpec(memory_space=pltpu.SMEM)
HBM = pl.BlockSpec(memory_space=pltpu.HBM)


def bytes_of(arrays):
    return sum(math.prod(a.shape) * a.dtype.itemsize for a in jax.tree.leaves(arrays))


def call(kernel, out_shape, scratch, mebibytes, flops, args, in_specs=None, out_specs=None):
    size = bytes_of((args, out_shape))
    return pl.pallas_call(
        kernel,
        out_shape=out_shape,
        in_specs=in_specs or [VMEM] * len(args),
        out_specs=out_specs or jax.tree.map(lambda _: VMEM, out_shape),
        scratch_shapes=scratch,
        compiler_params=pltpu.CompilerParams(vmem_limit_bytes=mebibytes * 2**20),
        cost_estimate=pl.CostEstimate(flops=flops, transcendentals=0, bytes_accessed=size),
    )(*args)


def turned(number, length):
    number = number.astype(F32)
    number = number - length * jnp.floor(number / length)
    return number * (2.0 * math.pi / length)


def write_fourier(fourier_ref, length, orders):
    tile = 128
    factor = 1.0 / math.sqrt(length)
    shape = (tile, orders)
    fine = turned(iota(shape, 0) * (iota(shape, 1) + 1), length)
    fine_cos, fine_sin = jnp.cos(fine), jnp.sin(fine)
    blocks = length // tile
    padded = -(-blocks // 8) * 8
    shape = (padded, orders)
    coarse = turned(iota(shape, 0) * tile * (iota(shape, 1) + 1), length)
    coarse_cos, coarse_sin = jnp.cos(coarse) * factor, jnp.sin(coarse) * factor
    for block in range(blocks):
        cosine = coarse_cos[block : block + 1, :]
        sine = coarse_sin[block : block + 1, :]
        rows = slice(block * tile, (block + 1) * tile)
        fourier_ref[rows, :orders] = (cosine * fine_cos - sine * fine_sin).astype(BF16)
        fourier_ref[rows, orders:] = (-(sine * fine_cos + cosine * fine_sin)).astype(BF16)


def write_spectra(send_ref, slot, real, imaginary):
    members, _, owned, _ = send_ref.shape
    flipped = jnp.concatenate([real, imaginary], axis=0).T
    for device in range(members):
        send_ref[device, slot] = flipped[device * owned : (device + 1) * owned, :].astype(BF16)


def taps_of(weight_ref, dx):
    return jnp.concatenate([weight_ref[dy, dx] for dy in range(weight_ref.shape[0])], axis=0)


def shifted_sum(partial_ref, rows, height, first, count):
    taps = rows // height
    radius = taps // 2
    total = None
    for dx in range(taps):
        start = dx * height + first
        piece = partial_ref[start : start + count, :]
        if dx != radius:
            piece = pltpu.roll(piece, (radius - dx) % piece.shape[1], 1)
        total = piece if total is None else total + piece
    return total


def picked(group, radius, groups, field_ref, crossing):
    block = field_ref.shape[0] // groups
    height = block // group
    depth = radius * group
    shape = (depth, block)
    place, column = iota(shape, 0), iota(shape, 1)
    far = (lax.axis_index("lat") + crossing) % 2 == 0
    row = place % radius + jnp.where(far, height - radius, 0)
    chosen = column == place // radius * height + row
    selector = chosen.astype(F32).astype(BF16)
    for g in range(groups):
        yield dot_nn(selector, field_ref[g * block : (g + 1) * block, :]).astype(BF16)


def cross_kernel(group, radius, groups, field_ref, kept_ref, *cross_refs):
    depth = radius * group
    slots = [(ref, at) for ref in cross_refs for at in range(ref.shape[0] // depth)]
    for (ref, at), rows in zip(slots, picked(group, radius, groups, field_ref, 1)):
        ref[at * depth : (at + 1) * depth, :] = rows
    kept_ref[...] = field_ref[...]


def pair_kernel(group, radius, groups, field_ref, pair_ref):
    depth = radius * group
    for g, rows in enumerate(picked(group, radius, groups, field_ref, 0)):
        pair_ref[g * depth : (g + 1) * depth, :] = rows


def interior_kernel(
    group, weight_ref, bias_ref, field_ref,
    edge_ref, rim_ref, fourier_ref, send_ref,
    band_ref, partial_ref, hidden_ref, spectra_ref, column_ref,
):
    taps = weight_ref.shape[0]
    radius = taps // 2
    channels = weight_ref.shape[3]
    groups = channels // group
    height = field_ref.shape[0] // channels
    orders = fourier_ref.shape[1] // 2
    inner = height - 2 * radius
    block = height * group
    rows = taps * block

    write_fourier(fourier_ref, field_ref.shape[1], orders)
    shape = (channels, channels)
    bias = jnp.where(iota(shape, 0) == iota(shape, 1), bias_ref[...], 0.0)
    column_ref[...] = jnp.broadcast_to(jnp.sum(bias, axis=1, keepdims=True), column_ref.shape)
    shape = (taps * group, height * block)
    place = iota(shape, 0)
    column = iota(shape, 1)
    out_row, column = column // block, column % block
    chosen = (place % group == column // height) & (place // group == column % height - out_row + radius)
    selector = chosen.astype(F32).astype(BF16)
    position = lax.axis_index("lat")
    parity = position % 2
    polar = (position == 0) | (position == lax.axis_size("lat") - 1)
    open_side = jnp.where(polar, 0.0, 1.0)
    depth = radius * group
    rim_shape = (taps * group, 2 * depth)
    rim_place = iota(rim_shape, 0)
    rim_column = iota(rim_shape, 1)
    same = rim_place % group == rim_column % depth // radius
    rim_row = rim_column % radius
    rim_rows = taps * radius * group
    for dx in range(taps):
        mine = taps_of(weight_ref, dx)
        spread = dot_tn(mine, selector).astype(BF16)
        for g in range(groups):
            for row in range(height):
                start = g * rows + dx * block + row * group
                band_ref[start : start + group, :] = spread[
                    g * group : (g + 1) * group, row * block : (row + 1) * block
                ]
        for which in range(2):
            side = 1 - parity if which == 0 else parity
            for row in range(radius):
                tap = rim_row - row + side * (taps - 1)
                own = same & (rim_column // depth == which) & (rim_place // group == tap)
                pick = jnp.where(own, 1.0 if which == 0 else open_side, 0.0)
                spread = dot_tn(mine, pick.astype(BF16)).astype(BF16)
                for g in range(groups):
                    start = (g * 2 + which) * rim_rows + (dx * radius + row) * group
                    rim_ref[start : start + group, :] = spread[g * group : (g + 1) * group, :]

    def per_group(g, carry):
        band = band_ref[pl.ds(pl.multiple_of(g * rows, 16), rows), :]
        field = field_ref[pl.ds(pl.multiple_of(g * block, 16), block), :]
        partial_ref[...] = dot_nn(band, field)
        mine = pl.ds(pl.multiple_of(g * group, 16), group)
        bias = column_ref[mine, :][:, :1]
        for row in range(height):
            total = shifted_sum(partial_ref, rows, block, row * group, group) + bias
            if radius <= row < height - radius:
                start = pl.multiple_of((row - radius) * channels + g * group, 16)
                hidden_ref[pl.ds(start, group), :] = gelu(total).astype(BF16)
            else:
                edge_ref[row if row < radius else row - inner, mine, :] = total
        return carry

    lax.fori_loop(0, groups, per_group, 0)

    found = dot_nn(jnp.concatenate([field_ref[...], hidden_ref[...]], axis=0), fourier_ref[...])
    pitch = height + 1
    total = pitch * channels
    for part in range(2):
        for channel in range(channels):
            start = part * total + channel * pitch
            spectra_ref[start : start + height, :] = found[
                channel * height : (channel + 1) * height, part * orders : (part + 1) * orders
            ]
    for row in range(height):
        real, imaginary = (
            spectra_ref[pl.ds(part * total + row, channels, stride=pitch), :] for part in range(2)
        )
        write_spectra(send_ref, row, real, imaginary)
    for row in range(inner):
        start = (height + row) * channels
        mine = found[start : start + channels, :]
        write_spectra(send_ref, height + row, mine[:, :orders], mine[:, orders:])


def write_rim(group, radius, groups, rim_ref, edge_ref, pair_ref, cross_ref, partial_ref, store):
    rows = partial_ref.shape[0]
    depth = radius * group
    parity = lax.axis_index("lat") % 2

    def per_group(at, carry):
        g = groups[0] + at
        rim = rim_ref[pl.ds(pl.multiple_of(g * rows, 16), rows), :]
        pair = pair_ref[pl.ds(pl.multiple_of(g * depth, 16), depth), :]
        cross = cross_ref[pl.ds(pl.multiple_of(at * depth, 16), depth), :]
        partial_ref[...] = dot_nn(rim, jnp.concatenate([pair, cross], axis=0))
        for which, side in ((0, 1 - parity), (1, parity)):
            mine_ref = partial_ref.at[which * rows // 2 : (which + 1) * rows // 2]
            for row in range(radius):
                total = shifted_sum(mine_ref, rows // 2, depth, row * group, group)
                place = side * radius + row
                total = total + edge_ref[place, pl.ds(pl.multiple_of(g * group, 16), group), :]
                store(place, g, at, gelu(total).astype(BF16))
        return carry

    lax.fori_loop(0, groups[1] - groups[0], per_group, 0)


def first_rim_kernel(group, radius, groups, rim_ref, edge_ref, pair_ref, cross_ref, hidden_ref, partial_ref):
    def store(place, g, at, value):
        hidden_ref[place, pl.ds(pl.multiple_of(at * group, 16), group), :] = value

    write_rim(group, radius, groups, rim_ref, edge_ref, pair_ref, cross_ref, partial_ref, store)


def last_rim_kernel(
    group, radius, groups, rim_ref, edge_ref, pair_ref, cross_ref, fourier_ref, early_ref, *refs
):
    before_refs, (send_hbm, partial_ref, hidden_ref, late_ref, semaphores) = refs[:-5], refs[-5:]
    channels = edge_ref.shape[1]
    orders = fourier_ref.shape[1] // 2
    early = early_ref.shape[1]
    first = pltpu.make_async_copy(early_ref, send_hbm.at[:, pl.ds(0, early)], semaphores.at[0])
    first.start()
    for place in range(2 * radius):
        for before_ref in before_refs:
            size = before_ref.shape[1]
            hidden_ref[place * channels : place * channels + size, :] = before_ref[place]

    def store(place, g, at, value):
        start = pl.multiple_of(place * channels + g * group, 16)
        hidden_ref[pl.ds(start, group), :] = value

    write_rim(group, radius, groups, rim_ref, edge_ref, pair_ref, cross_ref, partial_ref, store)
    found = dot_nn(hidden_ref[...], fourier_ref[...])
    for row in range(2 * radius):
        mine = found[row * channels : (row + 1) * channels, :]
        write_spectra(late_ref, row, mine[:, :orders], mine[:, orders:])
    last = pltpu.make_async_copy(late_ref, send_hbm.at[:, pl.ds(early, 2 * radius)], semaphores.at[1])
    last.start()
    first.wait()
    last.wait()


def tables_kernel(
    group, turn_ref, sphere_ref, weight_ref,
    table_ref,
    steps_ref, rate_ref, base_ref, turned_ref,
):
    taps = weight_ref.shape[0]
    radius = taps // 2
    channels = weight_ref.shape[3]
    degrees = rate_ref.shape[0] // 2
    owned = table_ref.shape[0]
    wide = 2 * channels
    head = sphere_ref.shape[1]
    places = head * LANES // owned
    first_order = lax.axis_index("lat") * owned + 1

    shape = (degrees, LANES)
    order = (iota(shape, 1) % owned + first_order).astype(F32)
    degree = iota(shape, 0).astype(F32)
    previous = degree - 1.0
    raising = jnp.sqrt(
        jnp.maximum(4.0 * degree * degree - 1.0, 1.0) / jnp.maximum(degree * degree - order * order, 1.0)
    )
    lowering = jnp.sqrt(
        jnp.maximum(previous * previous - order * order, 0.0)
        / jnp.maximum(4.0 * previous * previous - 1.0, 1.0)
    )
    rate_ref[:degrees, :] = raising
    rate_ref[degrees:, :] = lowering

    shape = (ORDERS, LANES)
    number = (iota(shape, 0) + 1).astype(F32)
    ratio = jnp.where(
        iota(shape, 0) < iota(shape, 1) % owned + first_order, jnp.log((2.0 * number - 1.0) / (2.0 * number)), 0.0
    )
    log_ratio = jnp.sum(ratio, axis=0, keepdims=True)
    shape = (head, LANES)
    whole_order = iota(shape, 1) % owned + first_order
    order = whole_order.astype(F32)
    cosine, log_sine, quadrature = sphere_ref[0], sphere_ref[1], sphere_ref[2]
    diagonal = jnp.exp(0.5 * (jnp.log((2.0 * order + 1.0) / 2.0) + log_ratio) + order * log_sine)

    twice = (iota((channels, wide), 1) % channels == iota((channels, wide), 0)).astype(F32).astype(BF16)
    across = (iota((group, wide), 1) % group == iota((group, wide), 0)).astype(F32).astype(BF16)
    shape = (wide, wide)
    row, column = iota(shape, 0), iota(shape, 1)
    row_part, column_part = row // channels, column // channels
    same_group = row % channels // group == column % channels // group
    straight = row_part == column_part
    sign = jnp.where(column_part > row_part, 1.0, -1.0)
    flat = jnp.concatenate([weight_ref[dy, dx] for dy in range(taps) for dx in range(taps)], axis=0)
    doubled = dot_nn(flat, twice).astype(BF16)

    def expanded(dy, dx):
        start = (dy * taps + dx) * group
        return dot_tn(across, doubled[start : start + group, :])

    for dy in range(taps):
        tap = [expanded(dy, dx) for dx in range(taps)]
        base_ref[dy, 0] = jnp.where(same_group & straight, tap[radius], 0.0)
        for far in range(1, radius + 1):
            high, low = tap[radius + far], tap[radius - far]
            both = jnp.where(straight, high + low, sign * (high - low))
            base_ref[dy, far] = jnp.where(same_group, both, 0.0)
    steps = degrees // owned

    def per_order(k, carried):
        latest, before = carried
        for step in range(steps):
            at = k * steps + step
            up = jnp.broadcast_to(rate_ref[pl.ds(at, 1), :], (head, LANES))
            down = jnp.broadcast_to(rate_ref[pl.ds(degrees + at, 1), :], (head, LANES))
            raised = up * (cosine * latest - down * before)
            latest, before = jnp.where(whole_order == at, diagonal, raised), latest
            steps_ref[pl.ds(pl.multiple_of(at * head, 8), head), :] = latest * quadrature
        factors = [
            jnp.where(straight, turn_ref[2 * far, k], turn_ref[2 * far + 1, k]) for far in range(radius)
        ]
        for dy in range(taps):
            total = base_ref[dy, 0]
            for far in range(radius):
                total = total + base_ref[dy, far + 1] * factors[far]
            table_ref[k, dy * wide : (dy + 1) * wide, :wide] = total.astype(BF16)
        return latest, before

    nothing = order * cosine * 0.0
    lax.fori_loop(0, owned, per_order, (nothing, nothing))
    half = degrees // 2
    total = head * LANES
    for parity in range(2):
        for at in range(head):
            mine = steps_ref[pl.ds(parity * head + at, half, stride=2 * head), :]
            turned_ref[parity * total + at * LANES : parity * total + (at + 1) * LANES, :] = mine.T
    for parity in range(2):
        for k in range(owned):
            mine = turned_ref[pl.ds(parity * total + k, places, stride=owned), :]
            start = taps * wide + parity * places
            table_ref[k, start : start + places, :half] = mine.astype(BF16)


def project_kernel(
    radius, got_ref, table_ref, out_hbm, rows_ref, plain_ref, out_ref, semaphores
):
    members, height, owned, wide = got_ref.shape
    height = height // 2
    places = members * height
    pitch = owned + 1
    pad = radius * pitch
    taps = 2 * radius + 1

    rows_ref[:pad, :] = jnp.zeros((pad, rows_ref.shape[1]), F32)
    rows_ref[pad + places * pitch :, :] = jnp.zeros((pad, rows_ref.shape[1]), F32)
    for source in range(members):
        for row in range(height):
            start = (source * height + row) * pitch
            plain_ref[start : start + owned, :wide] = got_ref[source, row].astype(F32)
            if radius <= row < height - radius:
                place = height + row - radius
            elif row < radius:
                place = 2 * height - 2 * radius + row
            else:
                place = height + row
            rows_ref[pad + start : pad + start + owned, :wide] = got_ref[source, place].astype(F32)

    mix = taps * wide
    half = out_ref.shape[3]
    channels = wide // 2

    def sent(k):
        return pltpu.make_async_copy(out_ref.at[k], out_hbm.at[k], semaphores.at[k])

    def gathered(k):
        pieces = [rows_ref[pl.ds(dy * pitch + k, places, stride=pitch), :] for dy in range(taps)]
        return jnp.concatenate([piece[:, :wide].astype(BF16) for piece in pieces], axis=1)

    together = 2 if owned % 2 == 0 else 1
    for first in range(0, owned, together):
        orders = range(first, first + together)
        stacked = jnp.concatenate([gathered(k) for k in orders], axis=0)
        mixing = jnp.concatenate([table_ref[k, :mix, :wide] for k in orders], axis=1)
        both = dot_nn(stacked, mixing)
        for at, k in enumerate(orders):
            mixed = both[at * places : (at + 1) * places, at * wide : (at + 1) * wide]
            mixed = (mixed + plain_ref[pl.ds(k, places, stride=pitch), :][:, :wide]).T.astype(BF16)
            legendre = jnp.concatenate(
                [table_ref[k, mix + q * places : mix + (q + 1) * places, :half] for q in range(2)], axis=1
            )
            found = dot_nn(mixed, legendre)
            for part in range(2):
                rows = pl.ds(part, channels, stride=2)
                mine = found[part * channels : (part + 1) * channels, :]
                out_ref[k, 0, rows, :] = mine[:, :half]
                out_ref[k, 1, rows, :] = mine[:, half:]
            sent(k).start()
    for k in range(owned):
        sent(k).wait()


def per_device(atmosphere, first_weight, first_bias, second_weight):
    members = lax.axis_size("lat")
    position = lax.axis_index("lat")
    channels, height, length = atmosphere.shape
    group, taps = first_weight.shape[1], first_weight.shape[3]
    radius = taps // 2
    groups = channels // group
    inner = height - 2 * radius
    owned = ORDERS // members
    wide = 2 * channels
    places = height * members

    shapes = jax.ShapeDtypeStruct
    block = height * group
    rim_rows = taps * radius * group
    first_taps = first_weight.transpose(2, 3, 1, 0)
    second_taps = second_weight.transpose(2, 3, 1, 0)
    flat = atmosphere.reshape(channels * height, length)
    share = -(-groups // 4)
    parts = [count for count in (groups - share, share) if count]
    flat, *crossed = call(
        lambda *refs: cross_kernel(group, radius, groups, *refs),
        (shapes(flat.shape, BF16),) + tuple(shapes((p * group * radius, length), BF16) for p in parts),
        [],
        6,
        2 * radius * channels * block * length,
        (flat,),
    )
    crosses = [(i, (i + 1 if i % 2 else i - 1) % members) for i in range(members)]
    for at, cross in enumerate(crossed):
        crossed[at] = lax.ppermute(cross, "lat", crosses)
    pair = call(
        lambda *refs: pair_kernel(group, radius, groups, *refs),
        shapes((channels * radius, length), BF16),
        [],
        6,
        2 * radius * channels * block * length,
        (flat,),
    )
    pairs = [(i, i ^ 1) for i in range(members) if i ^ 1 < members]
    pair = lax.ppermute(pair, "lat", pairs)

    edge, rim, fourier, early = call(
        lambda *refs: interior_kernel(group, *refs),
        (
            shapes((2 * radius, channels, length), F32),
            shapes((groups * 2 * rim_rows, 2 * radius * group), BF16),
            shapes((length, 2 * ORDERS), BF16),
            shapes((members, height + inner, owned, wide), BF16),
        ),
        [
            pltpu.VMEM((groups * taps * block, block), BF16),
            pltpu.VMEM((taps * block, length), F32),
            pltpu.VMEM((inner * channels, length), BF16),
            pltpu.VMEM((2 * (height + 1) * channels, ORDERS), F32),
            pltpu.VMEM((channels, LANES), F32),
        ],
        10,
        2 * taps * block * block * length * groups,
        (first_taps, first_bias[None, :], flat),
    )
    partial = pltpu.VMEM((2 * rim_rows, length), F32)
    flops = 8 * rim_rows * radius * group * length * share
    before = [
        call(
            lambda *refs: first_rim_kernel(group, radius, (0, groups - share), *refs),
            shapes((2 * radius, (groups - share) * group, length), BF16),
            [partial],
            6,
            flops,
            (rim, edge, pair, cross),
        )
        for cross in crossed[:-1]
    ]
    send = call(
        lambda *refs: last_rim_kernel(group, radius, (groups - share, groups), *refs),
        shapes((members, 2 * height, owned, wide), BF16),
        [
            partial,
            pltpu.VMEM((2 * radius * channels, length), BF16),
            pltpu.VMEM((members, 2 * radius, owned, wide), BF16),
            pltpu.SemaphoreType.DMA((2,)),
        ],
        8,
        flops,
        (rim, edge, pair, crossed[-1], fourier, early, *before),
        out_specs=HBM,
    )
    got = lax.all_to_all(send, "lat", 0, 0, tiled=True)

    angle = (position * owned + 1 + jnp.arange(owned, dtype=jnp.int32)).astype(F32) * (2.0 * math.pi / length)
    turns = jnp.stack([f(far * angle) for far in range(1, radius + 1) for f in (jnp.cos, jnp.sin)])
    colatitude = np.pi * (np.arange(places) + 0.5) / places
    cosine = np.cos(colatitude)
    cosine[places // 2 :] = -cosine[: places // 2][::-1]
    sine = np.sin(np.minimum(colatitude, colatitude[::-1]))
    sphere = np.stack([cosine, np.log(sine), np.pi * sine / np.sqrt(places)]).astype(np.float32)
    head = places * owned // LANES
    sphere = np.repeat(sphere.reshape(3, head, LANES // owned), owned, axis=2)
    table = call(
        lambda *refs: tables_kernel(group, *refs),
        shapes((owned, taps * wide + 2 * places, max(wide, DEGREES // 2)), BF16),
        [
            pltpu.VMEM((DEGREES * head, LANES), F32),
            pltpu.VMEM((2 * DEGREES, LANES), F32),
            pltpu.VMEM((taps, radius + 1, wide, wide), F32),
            pltpu.VMEM((2 * head * LANES, DEGREES // 2), F32),
        ],
        6,
        2 * owned * wide * taps * wide * 8,
        (turns, jnp.asarray(sphere), second_taps),
        in_specs=[SMEM, VMEM, VMEM],
    )

    lanes = max(wide, LANES)
    spectrum = call(
        lambda *refs: project_kernel(radius, *refs),
        shapes((owned, 2, wide, DEGREES // 2), F32),
        [
            pltpu.VMEM(((places + 2 * radius) * (owned + 1), lanes), F32),
            pltpu.VMEM((places * (owned + 1), lanes), F32),
            pltpu.VMEM((owned, 2, wide, DEGREES // 2), F32),
            pltpu.SemaphoreType.DMA((owned,)),
        ],
        6,
        2 * owned * wide * places * ((taps + 1) * wide + DEGREES),
        (got, table),
        out_specs=HBM,
    )
    return spectrum.reshape(owned, 2, channels, 2, DEGREES // 2)


def solution(mesh):
    placed = (
        P("chan", "lat", None),
        P("chan", None, None, None),
        P("chan"),
        P("chan", None, None, None),
    )

    return jax.shard_map(
        per_device,
        mesh=mesh,
        in_specs=placed,
        out_specs=P("lat", None, "chan", None, None),
        check_vma=False,
    )
```

```python
import math

import jax
import jax.numpy as jnp
import numpy as np
from jax import lax
from jax.experimental import pallas as pl
from jax.experimental.pallas import tpu as pltpu
from jax.sharding import PartitionSpec as P

ORDERS = 128
DEGREES = 256
LANES = 128
F32 = jnp.float32
BF16 = jnp.bfloat16


def dot_tn(left, right):
    return lax.dot_general(left, right, (((0,), (0,)), ((), ())), preferred_element_type=F32)


def dot_nn(left, right):
    return jnp.dot(left, right, preferred_element_type=F32)


def iota(shape, dim):
    return lax.broadcasted_iota(jnp.int32, shape, dim)


def gelu(value):
    return 0.5 * value * (1.0 + lax.erf(value * math.sqrt(0.5)))


VMEM = pl.BlockSpec(memory_space=pltpu.VMEM)
SMEM = pl.BlockSpec(memory_space=pltpu.SMEM)
HBM = pl.BlockSpec(memory_space=pltpu.HBM)


def bytes_of(arrays):
    return sum(math.prod(a.shape) * a.dtype.itemsize for a in jax.tree.leaves(arrays))


def call(kernel, out_shape, scratch, mebibytes, flops, args, in_specs=None, out_specs=None):
    size = bytes_of((args, out_shape))
    return pl.pallas_call(
        kernel,
        out_shape=out_shape,
        in_specs=in_specs or [VMEM] * len(args),
        out_specs=out_specs or jax.tree.map(lambda _: VMEM, out_shape),
        scratch_shapes=scratch,
        compiler_params=pltpu.CompilerParams(vmem_limit_bytes=mebibytes * 2**20),
        cost_estimate=pl.CostEstimate(flops=flops, transcendentals=0, bytes_accessed=size),
    )(*args)


def turned(number, length):
    number = number.astype(F32)
    number = number - length * jnp.floor(number / length)
    return number * (2.0 * math.pi / length)


def write_fourier(fourier_ref, length, orders):
    tile = 128
    factor = 1.0 / math.sqrt(length)
    shape = (tile, orders)
    fine = turned(iota(shape, 0) * (iota(shape, 1) + 1), length)
    fine_cos, fine_sin = jnp.cos(fine), jnp.sin(fine)
    blocks = length // tile
    padded = -(-blocks // 8) * 8
    shape = (padded, orders)
    coarse = turned(iota(shape, 0) * tile * (iota(shape, 1) + 1), length)
    coarse_cos, coarse_sin = jnp.cos(coarse) * factor, jnp.sin(coarse) * factor
    for block in range(blocks):
        cosine = coarse_cos[block : block + 1, :]
        sine = coarse_sin[block : block + 1, :]
        rows = slice(block * tile, (block + 1) * tile)
        fourier_ref[rows, :orders] = (cosine * fine_cos - sine * fine_sin).astype(BF16)
        fourier_ref[rows, orders:] = (-(sine * fine_cos + cosine * fine_sin)).astype(BF16)


def write_spectra(send_ref, slot, real, imaginary):
    members, _, owned, _ = send_ref.shape
    flipped = jnp.concatenate([real, imaginary], axis=0).T
    for device in range(members):
        send_ref[device, slot] = flipped[device * owned : (device + 1) * owned, :].astype(BF16)


def taps_of(weight_ref, dx):
    return jnp.concatenate([weight_ref[dy, dx] for dy in range(weight_ref.shape[0])], axis=0)


def shifted_sum(partial_ref, rows, height, first, count):
    taps = rows // height
    radius = taps // 2
    total = None
    for dx in range(taps):
        start = dx * height + first
        piece = partial_ref[start : start + count, :]
        if dx != radius:
            piece = pltpu.roll(piece, (radius - dx) % piece.shape[1], 1)
        total = piece if total is None else total + piece
    return total


def picked(group, radius, groups, field_ref, crossing):
    block = field_ref.shape[0] // groups
    height = block // group
    depth = radius * group
    shape = (depth, block)
    place, column = iota(shape, 0), iota(shape, 1)
    far = (lax.axis_index("lat") + crossing) % 2 == 0
    row = place % radius + jnp.where(far, height - radius, 0)
    chosen = column == place // radius * height + row
    selector = chosen.astype(F32).astype(BF16)
    for g in range(groups):
        yield dot_nn(selector, field_ref[g * block : (g + 1) * block, :]).astype(BF16)


def cross_kernel(group, radius, groups, field_ref, kept_ref, *cross_refs):
    depth = radius * group
    slots = [(ref, at) for ref in cross_refs for at in range(ref.shape[0] // depth)]
    for (ref, at), rows in zip(slots, picked(group, radius, groups, field_ref, 1)):
        ref[at * depth : (at + 1) * depth, :] = rows
    kept_ref[...] = field_ref[...]


def pair_kernel(group, radius, groups, field_ref, pair_ref):
    depth = radius * group
    for g, rows in enumerate(picked(group, radius, groups, field_ref, 0)):
        pair_ref[g * depth : (g + 1) * depth, :] = rows


def interior_kernel(
    group, weight_ref, bias_ref, field_ref,
    edge_ref, rim_ref, fourier_ref, send_ref,
    band_ref, partial_ref, hidden_ref, spectra_ref, column_ref,
):
    taps = weight_ref.shape[0]
    radius = taps // 2
    channels = weight_ref.shape[3]
    groups = channels // group
    height = field_ref.shape[0] // channels
    orders = fourier_ref.shape[1] // 2
    inner = height - 2 * radius
    block = height * group
    rows = taps * block

    write_fourier(fourier_ref, field_ref.shape[1], orders)
    shape = (channels, channels)
    bias = jnp.where(iota(shape, 0) == iota(shape, 1), bias_ref[...], 0.0)
    column_ref[...] = jnp.broadcast_to(jnp.sum(bias, axis=1, keepdims=True), column_ref.shape)
    shape = (taps * group, height * block)
    place = iota(shape, 0)
    column = iota(shape, 1)
    out_row, column = column // block, column % block
    chosen = (place % group == column // height) & (place // group == column % height - out_row + radius)
    selector = chosen.astype(F32).astype(BF16)
    position = lax.axis_index("lat")
    parity = position % 2
    polar = (position == 0) | (position == lax.axis_size("lat") - 1)
    open_side = jnp.where(polar, 0.0, 1.0)
    depth = radius * group
    rim_shape = (taps * group, 2 * depth)
    rim_place = iota(rim_shape, 0)
    rim_column = iota(rim_shape, 1)
    same = rim_place % group == rim_column % depth // radius
    rim_row = rim_column % radius
    rim_rows = taps * radius * group
    for dx in range(taps):
        mine = taps_of(weight_ref, dx)
        spread = dot_tn(mine, selector).astype(BF16)
        for g in range(groups):
            for row in range(height):
                start = g * rows + dx * block + row * group
                band_ref[start : start + group, :] = spread[
                    g * group : (g + 1) * group, row * block : (row + 1) * block
                ]
        for which in range(2):
            side = 1 - parity if which == 0 else parity
            for row in range(radius):
                tap = rim_row - row + side * (taps - 1)
                own = same & (rim_column // depth == which) & (rim_place // group == tap)
                pick = jnp.where(own, 1.0 if which == 0 else open_side, 0.0)
                spread = dot_tn(mine, pick.astype(BF16)).astype(BF16)
                for g in range(groups):
                    start = (g * 2 + which) * rim_rows + (dx * radius + row) * group
                    rim_ref[start : start + group, :] = spread[g * group : (g + 1) * group, :]

    def per_group(g, carry):
        band = band_ref[pl.ds(pl.multiple_of(g * rows, 16), rows), :]
        field = field_ref[pl.ds(pl.multiple_of(g * block, 16), block), :]
        partial_ref[...] = dot_nn(band, field)
        mine = pl.ds(pl.multiple_of(g * group, 16), group)
        bias = column_ref[mine, :][:, :1]
        for row in range(height):
            total = shifted_sum(partial_ref, rows, block, row * group, group) + bias
            if radius <= row < height - radius:
                start = pl.multiple_of((row - radius) * channels + g * group, 16)
                hidden_ref[pl.ds(start, group), :] = gelu(total).astype(BF16)
            else:
                edge_ref[row if row < radius else row - inner, mine, :] = total
        return carry

    lax.fori_loop(0, groups, per_group, 0)

    found = dot_nn(field_ref[...], fourier_ref[...])
    pitch = height + 1
    total = pitch * channels
    for part in range(2):
        for channel in range(channels):
            start = part * total + channel * pitch
            spectra_ref[start : start + height, :] = found[
                channel * height : (channel + 1) * height, part * orders : (part + 1) * orders
            ]
    for row in range(height):
        real, imaginary = (
            spectra_ref[pl.ds(part * total + row, channels, stride=pitch), :] for part in range(2)
        )
        write_spectra(send_ref, row, real, imaginary)
    found = dot_nn(hidden_ref[...], fourier_ref[...])
    for row in range(inner):
        mine = found[row * channels : (row + 1) * channels, :]
        write_spectra(send_ref, height + row, mine[:, :orders], mine[:, orders:])


def write_rim(group, radius, groups, rim_ref, edge_ref, pair_ref, cross_ref, partial_ref, store):
    rows = partial_ref.shape[0]
    depth = radius * group
    parity = lax.axis_index("lat") % 2

    def per_group(at, carry):
        g = groups[0] + at
        rim = rim_ref[pl.ds(pl.multiple_of(g * rows, 16), rows), :]
        pair = pair_ref[pl.ds(pl.multiple_of(g * depth, 16), depth), :]
        cross = cross_ref[pl.ds(pl.multiple_of(at * depth, 16), depth), :]
        partial_ref[...] = dot_nn(rim, jnp.concatenate([pair, cross], axis=0))
        for which, side in ((0, 1 - parity), (1, parity)):
            mine_ref = partial_ref.at[which * rows // 2 : (which + 1) * rows // 2]
            for row in range(radius):
                total = shifted_sum(mine_ref, rows // 2, depth, row * group, group)
                place = side * radius + row
                total = total + edge_ref[place, pl.ds(pl.multiple_of(g * group, 16), group), :]
                store(place, g, at, gelu(total).astype(BF16))
        return carry

    lax.fori_loop(0, groups[1] - groups[0], per_group, 0)


def first_rim_kernel(
    group, radius, groups, rim_ref, edge_ref, pair_ref, cross_ref, fourier_ref, found_ref, partial_ref, hidden_ref
):
    size = found_ref.shape[1]

    def store(place, g, at, value):
        hidden_ref[pl.ds(pl.multiple_of(place * size + at * group, 16), group), :] = value

    write_rim(group, radius, groups, rim_ref, edge_ref, pair_ref, cross_ref, partial_ref, store)
    found = dot_nn(hidden_ref[...], fourier_ref[...])
    for place in range(2 * radius):
        found_ref[place] = found[place * size : (place + 1) * size, :]


def last_rim_kernel(
    group, radius, groups, rim_ref, edge_ref, pair_ref, cross_ref, fourier_ref, early_ref, *refs
):
    before_refs, (send_hbm, partial_ref, hidden_ref, late_ref, semaphores) = refs[:-5], refs[-5:]
    orders = fourier_ref.shape[1] // 2
    early = early_ref.shape[1]
    first = pltpu.make_async_copy(early_ref, send_hbm.at[:, pl.ds(0, early)], semaphores.at[0])
    first.start()
    size = hidden_ref.shape[0] // (2 * radius)

    def store(place, g, at, value):
        start = pl.multiple_of(place * size + at * group, 16)
        hidden_ref[pl.ds(start, group), :] = value

    write_rim(group, radius, groups, rim_ref, edge_ref, pair_ref, cross_ref, partial_ref, store)
    found = dot_nn(hidden_ref[...], fourier_ref[...])
    for row in range(2 * radius):
        mine = [before_ref[row] for before_ref in before_refs] + [found[row * size : (row + 1) * size, :]]
        mine = jnp.concatenate(mine, axis=0)
        write_spectra(late_ref, row, mine[:, :orders], mine[:, orders:])
    last = pltpu.make_async_copy(late_ref, send_hbm.at[:, pl.ds(early, 2 * radius)], semaphores.at[1])
    last.start()
    first.wait()
    last.wait()


def tables_kernel(
    group, turn_ref, sphere_ref, weight_ref,
    table_ref,
    steps_ref, rate_ref, base_ref, turned_ref,
):
    taps = weight_ref.shape[0]
    radius = taps // 2
    channels = weight_ref.shape[3]
    degrees = rate_ref.shape[0] // 2
    owned = table_ref.shape[0]
    wide = 2 * channels
    head = sphere_ref.shape[1]
    places = head * LANES // owned
    first_order = lax.axis_index("lat") * owned + 1

    shape = (degrees, LANES)
    order = (iota(shape, 1) % owned + first_order).astype(F32)
    degree = iota(shape, 0).astype(F32)
    previous = degree - 1.0
    raising = jnp.sqrt(
        jnp.maximum(4.0 * degree * degree - 1.0, 1.0) / jnp.maximum(degree * degree - order * order, 1.0)
    )
    lowering = jnp.sqrt(
        jnp.maximum(previous * previous - order * order, 0.0)
        / jnp.maximum(4.0 * previous * previous - 1.0, 1.0)
    )
    rate_ref[:degrees, :] = raising
    rate_ref[degrees:, :] = lowering

    shape = (ORDERS, LANES)
    number = (iota(shape, 0) + 1).astype(F32)
    ratio = jnp.where(
        iota(shape, 0) < iota(shape, 1) % owned + first_order, jnp.log((2.0 * number - 1.0) / (2.0 * number)), 0.0
    )
    log_ratio = jnp.sum(ratio, axis=0, keepdims=True)
    shape = (head, LANES)
    whole_order = iota(shape, 1) % owned + first_order
    order = whole_order.astype(F32)
    cosine, log_sine, quadrature = sphere_ref[0], sphere_ref[1], sphere_ref[2]
    diagonal = jnp.exp(0.5 * (jnp.log((2.0 * order + 1.0) / 2.0) + log_ratio) + order * log_sine)

    twice = (iota((channels, wide), 1) // 2 == iota((channels, wide), 0)).astype(F32).astype(BF16)
    across = (iota((group, wide), 1) % group == iota((group, wide), 0)).astype(F32).astype(BF16)
    shape = (wide, wide)
    row, column = iota(shape, 0), iota(shape, 1)
    row_part, column_part = row // channels, column % 2
    same_group = row % channels // group == column // 2 // group
    straight = row_part == column_part
    sign = jnp.where(column_part > row_part, 1.0, -1.0)
    flat = jnp.concatenate([weight_ref[dy, dx] for dy in range(taps) for dx in range(taps)], axis=0)
    doubled = dot_nn(flat, twice).astype(BF16)

    def expanded(dy, dx):
        start = (dy * taps + dx) * group
        return dot_tn(across, doubled[start : start + group, :])

    for dy in range(taps):
        tap = [expanded(dy, dx) for dx in range(taps)]
        base_ref[dy, 0] = jnp.where(same_group & straight, tap[radius], 0.0)
        for far in range(1, radius + 1):
            high, low = tap[radius + far], tap[radius - far]
            both = jnp.where(straight, high + low, sign * (high - low))
            base_ref[dy, far] = jnp.where(same_group, both, 0.0)
    steps = degrees // owned

    def per_order(k, carried):
        latest, before = carried
        for step in range(steps):
            at = k * steps + step
            up = jnp.broadcast_to(rate_ref[pl.ds(at, 1), :], (head, LANES))
            down = jnp.broadcast_to(rate_ref[pl.ds(degrees + at, 1), :], (head, LANES))
            raised = up * (cosine * latest - down * before)
            latest, before = jnp.where(whole_order == at, diagonal, raised), latest
            steps_ref[pl.ds(pl.multiple_of(at * head, 8), head), :] = latest * quadrature
        factors = [
            jnp.where(straight, turn_ref[2 * far, k], turn_ref[2 * far + 1, k]) for far in range(radius)
        ]
        for dy in range(taps):
            total = base_ref[dy, 0]
            for far in range(radius):
                total = total + base_ref[dy, far + 1] * factors[far]
            table_ref[k, dy * wide : (dy + 1) * wide, :wide] = total.astype(BF16)
        return latest, before

    nothing = order * cosine * 0.0
    lax.fori_loop(0, owned, per_order, (nothing, nothing))
    half = degrees // 2
    total = head * LANES
    for parity in range(2):
        for at in range(head):
            mine = steps_ref[pl.ds(parity * head + at, half, stride=2 * head), :]
            turned_ref[parity * total + at * LANES : parity * total + (at + 1) * LANES, :] = mine.T
    for parity in range(2):
        for k in range(owned):
            mine = turned_ref[pl.ds(parity * total + k, places, stride=owned), :]
            start = taps * wide + parity * places
            table_ref[k, start : start + places, :half] = mine.astype(BF16)


def project_kernel(
    radius, got_ref, table_ref, out_hbm, rows_ref, plain_ref, out_ref, semaphores
):
    members, height, owned, wide = got_ref.shape
    height = height // 2
    places = members * height
    pitch = owned + 1
    pad = radius * pitch
    taps = 2 * radius + 1

    rows_ref[:pad, :] = jnp.zeros((pad, rows_ref.shape[1]), F32)
    rows_ref[pad + places * pitch :, :] = jnp.zeros((pad, rows_ref.shape[1]), F32)
    for source in range(members):
        for row in range(height):
            start = (source * height + row) * pitch
            plain_ref[start : start + owned, :wide] = got_ref[source, row].astype(F32)
            if radius <= row < height - radius:
                place = height + row - radius
            elif row < radius:
                place = 2 * height - 2 * radius + row
            else:
                place = height + row
            rows_ref[pad + start : pad + start + owned, :wide] = got_ref[source, place].astype(F32)

    row, column = iota((wide, wide), 0), iota((wide, wide), 1)
    identity = (row == column % 2 * (wide // 2) + column // 2).astype(F32).astype(BF16)
    identity = jnp.concatenate([identity] * (2 if owned % 2 == 0 else 1), axis=1)
    mix = taps * wide
    half = out_ref.shape[3]

    def sent(k):
        return pltpu.make_async_copy(out_ref.at[k], out_hbm.at[k], semaphores.at[k])

    def gathered(k):
        pieces = [rows_ref[pl.ds(dy * pitch + k, places, stride=pitch), :] for dy in range(taps)]
        pieces.append(plain_ref[pl.ds(k, places, stride=pitch), :])
        return jnp.concatenate([piece[:, :wide].astype(BF16) for piece in pieces], axis=1)

    together = 2 if owned % 2 == 0 else 1
    for first in range(0, owned, together):
        orders = range(first, first + together)
        stacked = jnp.concatenate([gathered(k) for k in orders], axis=0)
        mixing = jnp.concatenate([table_ref[k, :mix, :wide] for k in orders], axis=1)
        mixing = jnp.concatenate([mixing, identity], axis=0)
        both = dot_nn(stacked, mixing)
        for at, k in enumerate(orders):
            mixed = both[at * places : (at + 1) * places, at * wide : (at + 1) * wide].T.astype(BF16)
            legendre = jnp.concatenate(
                [table_ref[k, mix + q * places : mix + (q + 1) * places, :half] for q in range(2)], axis=1
            )
            found = dot_nn(mixed, legendre)
            out_ref[k, 0] = found[:, :half]
            out_ref[k, 1] = found[:, half:]
            sent(k).start()
    for k in range(owned):
        sent(k).wait()


def per_device(atmosphere, first_weight, first_bias, second_weight):
    members = lax.axis_size("lat")
    position = lax.axis_index("lat")
    channels, height, length = atmosphere.shape
    group, taps = first_weight.shape[1], first_weight.shape[3]
    radius = taps // 2
    groups = channels // group
    inner = height - 2 * radius
    owned = ORDERS // members
    wide = 2 * channels
    places = height * members

    shapes = jax.ShapeDtypeStruct
    block = height * group
    rim_rows = taps * radius * group
    first_taps = first_weight.transpose(2, 3, 1, 0)
    second_taps = second_weight.transpose(2, 3, 1, 0)
    flat = atmosphere.reshape(channels * height, length)
    share = -(-groups // 4)
    parts = [count for count in (groups - share, share) if count]
    flat, *crossed = call(
        lambda *refs: cross_kernel(group, radius, groups, *refs),
        (shapes(flat.shape, BF16),) + tuple(shapes((p * group * radius, length), BF16) for p in parts),
        [],
        6,
        2 * radius * channels * block * length,
        (flat,),
    )
    crosses = [(i, (i + 1 if i % 2 else i - 1) % members) for i in range(members)]
    for at, cross in enumerate(crossed):
        crossed[at] = lax.ppermute(cross, "lat", crosses)
    pair = call(
        lambda *refs: pair_kernel(group, radius, groups, *refs),
        shapes((channels * radius, length), BF16),
        [],
        6,
        2 * radius * channels * block * length,
        (flat,),
    )
    pairs = [(i, i ^ 1) for i in range(members) if i ^ 1 < members]
    pair = lax.ppermute(pair, "lat", pairs)

    edge, rim, fourier, early = call(
        lambda *refs: interior_kernel(group, *refs),
        (
            shapes((2 * radius, channels, length), F32),
            shapes((groups * 2 * rim_rows, 2 * radius * group), BF16),
            shapes((length, 2 * ORDERS), BF16),
            shapes((members, height + inner, owned, wide), BF16),
        ),
        [
            pltpu.VMEM((groups * taps * block, block), BF16),
            pltpu.VMEM((taps * block, length), F32),
            pltpu.VMEM((inner * channels, length), BF16),
            pltpu.VMEM((2 * (height + 1) * channels, ORDERS), F32),
            pltpu.VMEM((channels, LANES), F32),
        ],
        10,
        2 * taps * block * block * length * groups,
        (first_taps, first_bias[None, :], flat),
    )
    partial = pltpu.VMEM((2 * rim_rows, length), F32)
    flops = 8 * rim_rows * radius * group * length * share
    before = [
        call(
            lambda *refs: first_rim_kernel(group, radius, (0, groups - share), *refs),
            shapes((2 * radius, (groups - share) * group, 2 * ORDERS), F32),
            [partial, pltpu.VMEM((2 * radius * (groups - share) * group, length), BF16)],
            6,
            flops,
            (rim, edge, pair, cross, fourier),
        )
        for cross in crossed[:-1]
    ]
    send = call(
        lambda *refs: last_rim_kernel(group, radius, (groups - share, groups), *refs),
        shapes((members, 2 * height, owned, wide), BF16),
        [
            partial,
            pltpu.VMEM((2 * radius * share * group, length), BF16),
            pltpu.VMEM((members, 2 * radius, owned, wide), BF16),
            pltpu.SemaphoreType.DMA((2,)),
        ],
        8,
        flops,
        (rim, edge, pair, crossed[-1], fourier, early, *before),
        out_specs=HBM,
    )
    got = lax.all_to_all(send, "lat", 0, 0, tiled=True)

    angle = (position * owned + 1 + jnp.arange(owned, dtype=jnp.int32)).astype(F32) * (2.0 * math.pi / length)
    turns = jnp.stack([f(far * angle) for far in range(1, radius + 1) for f in (jnp.cos, jnp.sin)])
    colatitude = np.pi * (np.arange(places) + 0.5) / places
    cosine = np.cos(colatitude)
    cosine[places // 2 :] = -cosine[: places // 2][::-1]
    sine = np.sin(np.minimum(colatitude, colatitude[::-1]))
    sphere = np.stack([cosine, np.log(sine), np.pi * sine / np.sqrt(places)]).astype(np.float32)
    head = places * owned // LANES
    sphere = np.repeat(sphere.reshape(3, head, LANES // owned), owned, axis=2)
    table = call(
        lambda *refs: tables_kernel(group, *refs),
        shapes((owned, taps * wide + 2 * places, max(wide, DEGREES // 2)), BF16),
        [
            pltpu.VMEM((DEGREES * head, LANES), F32),
            pltpu.VMEM((2 * DEGREES, LANES), F32),
            pltpu.VMEM((taps, radius + 1, wide, wide), F32),
            pltpu.VMEM((2 * head * LANES, DEGREES // 2), F32),
        ],
        6,
        2 * owned * wide * taps * wide * 8,
        (turns, jnp.asarray(sphere), second_taps),
        in_specs=[SMEM, VMEM, VMEM],
    )

    lanes = max(wide, LANES)
    spectrum = call(
        lambda *refs: project_kernel(radius, *refs),
        shapes((owned, 2, wide, DEGREES // 2), F32),
        [
            pltpu.VMEM(((places + 2 * radius) * (owned + 1), lanes), F32),
            pltpu.VMEM((places * (owned + 1), lanes), F32),
            pltpu.VMEM((owned, 2, wide, DEGREES // 2), F32),
            pltpu.SemaphoreType.DMA((owned,)),
        ],
        6,
        2 * owned * wide * places * ((taps + 1) * wide + DEGREES),
        (got, table),
        out_specs=HBM,
    )
    return spectrum.reshape(owned, 2, channels, 2, DEGREES // 2)


def solution(mesh):
    placed = (
        P("chan", "lat", None),
        P("chan", None, None, None),
        P("chan"),
        P("chan", None, None, None),
    )

    return jax.shard_map(
        per_device,
        mesh=mesh,
        in_specs=placed,
        out_specs=P("lat", None, "chan", None, None),
        check_vma=False,
    )
```
